32 devices in a mesh: dp: 2 (over core), expert: 4 (over y, x), tensor: 4 (over z).
Axes of the slice: x: 2, y: 2, z: 4, core: 2. Of those that a mesh axis runs over, the one named last changes fastest.
Arguments:
- tokens: bfloat16 [16384, 768], P(('dp', 'expert')), may hold values from -6 to 6
- prev_logits: float32 [16384, 12], P(('dp', 'expert')), may hold values from -3 to 3
- routes: int32 [16384, 2], P(('dp', 'expert')), may hold values from 0 to 11, all different within a row; in each aligned block of 2048 rows (0 to 2047, 2048 to 4095, ...) at most 480 rows name the same one
- segments: int32 [16384], P(('dp', 'expert')), may hold values from 0 to 15, as said below
- gain_one: float32 [768], P('dp'), may hold values from 0.5 to 1.5
- w_qkv: float32 [768, 3, 768], P('dp', None, 'tensor'), may hold values from -0.21875 to 0.21875
- w_out: float32 [768, 768], P('tensor', 'dp'), may hold values from -0.875 to 0.875
- gain_two: float32 [768], P('dp'), may hold values from 0.5 to 1.5
- router: float32 [768, 12], P('dp'), may hold values from -0.109375 to 0.109375
- const_proj: float32 [768, 4], P('dp'), may hold values from -0.21875 to 0.21875
- const_vec: float32 [2, 768], P(None, 'dp'), may hold values from -6 to 6
- w_gate_up: float32 [8, 768, 2, 2048], P('expert', 'dp', None, 'tensor'), may hold values from -0.21875 to 0.21875
- w_down: float32 [8, 2048, 768], P('expert', 'tensor', 'dp'), may hold values from -2 to 2
- cotangent: bfloat16 [16384, 768], P(('dp', 'expert')), may hold values from -6 to 6
Outputs:
- output: float32 [16384, 768], P(('dp', 'expert'))
- grad_tokens: float32 [16384, 768], P(('dp', 'expert'))
- grad_gain_one: float32 [768], P('dp')
- grad_w_qkv: float32 [768, 3, 768], P('dp', None, 'tensor')
- grad_w_out: float32 [768, 768], P('tensor', 'dp')
- grad_gain_two: float32 [768], P('dp')
- grad_router: float32 [768, 12], P('dp')
- grad_const_proj: float32 [768, 4], P('dp')
- grad_const_vec: float32 [2, 768], P(None, 'dp')
- grad_w_gate_up: float32 [8, 768, 2, 2048], P('expert', 'dp', None, 'tensor')
- grad_w_down: float32 [8, 2048, 768], P('expert', 'tensor', 'dp')
The draws below stay inside these ranges and needn't reach their ends.
Inputs may be any that keep to these rules, and one draw needn't show every extreme that they name: `routes`: ids below 8 name expert networks, 8 the zero expert, 9 the copy expert, 10 and 11 the constant experts; a token's two ids differ; in the 2048 rows of one device no id is named more than 480 times. `segments`: within each sequence of 1024 tokens the numbers start at 0 and rise by one at each document start; documents start only at multiples of 64 and hold 64 to 768 tokens; the first sequence holds one of 768 tokens, and the last holds documents of 64 tokens only.
All inputs are finite; a program needn't handle non-finite values.
Results may differ from the reference program's by a relative error of at most 0.025.
Values may be sent and summed in bfloat16 or wider, within the bound.
No kernel may reach another device: no remote copies, remote signals or barrier semaphores. Data moves between devices by JAX's collectives and lax.ppermute only.
A program may use at most 256 MiB of HBM per device.

```python
import math
import jax
import jax.numpy as jnp
import numpy as np
from jax import lax

D = 768
HEADS = 12
HD = 64
FF = 2048
EXPERTS = 8
ALL_EXPERTS = 12
DOC_BLOCK = 64
SEQ_LEN = 1024
SEQS = 2
ROWS = 2048
TOKENS = 16384
CAPACITY = 480
N_DP = 2
N_EXPERT = 4
N_TENSOR = 4


def draw_segments(key, part):
    seq_total = TOKENS // SEQ_LEN
    block_total = SEQ_LEN // DOC_BLOCK
    starts = (jax.random.randint(key, (seq_total, block_total), 0, 5) < 2).astype(jnp.int32)
    columns = jnp.arange(block_total, dtype=jnp.int32)[None, :]
    sequence_ids = jnp.arange(seq_total, dtype=jnp.int32)[:, None]
    starts = jnp.where((columns == 0) | (columns == 12), 1, starts)
    starts = jnp.where((sequence_ids == 0) & (columns > 0) & (columns < 12), 0, starts)
    starts = jnp.where((sequence_ids == seq_total - 1) & (sequence_ids > 0), 1, starts)
    numbers = jnp.cumsum(starts, axis=1) - 1
    return jnp.repeat(numbers, DOC_BLOCK, axis=1).reshape(-1).astype(jnp.int32)


def steps_of(own_key, extent, shards, smallest, high):
    def one(position, blocks):
        draws = jax.random.uniform(jax.random.fold_in(jax.random.fold_in(own_key, 6), position), (blocks,), jnp.float32, smallest / len(shards), high / len(shards))
        return jnp.repeat(jnp.exp(draws), extent[position] // blocks).reshape((-1,) + (1,) * (len(extent) - position - 1))

    loudness = one(*shards[0])
    for cut in shards[1:]:
        loudness = loudness * one(*cut)
    return loudness


def deal_out(key, own, number, rows, count, top, limit, skew):
    order = jax.random.permutation(key, count)
    crowded, ordinary = portions_of(count, rows * top, limit, skew, True), portions_of(count, rows * top, limit, skew, False)
    places = jnp.arange(count)

    def named(tallies, rotation):
        used = int((tallies > 0).sum())
        fixed = max(1, used // 4)
        shifted = fixed + (places - fixed + rotation * (used - fixed)) % max(1, count - fixed)
        return jnp.zeros((count,), jnp.int32).at[order[jnp.where(places < fixed, places, shifted)]].set(jnp.asarray(tallies, jnp.int32))

    tallies = jnp.where(number % 4 == 0, named(crowded, number // 4), named(ordinary, number - number // 4 - 1))
    mixed = jax.random.permutation(jax.random.fold_in(own, 3), count)
    donor, receiver = mixed[0:count // 2 * 2:2], mixed[1:count // 2 * 2:2]
    slack = jnp.minimum(tallies[donor] - 1, limit - tallies[receiver]) // 2
    slack = jnp.where((donor == order[0]) | (receiver == order[0]) | (tallies[receiver] == 0), 0, jnp.maximum(slack, 0))
    shifted = jax.random.randint(jax.random.fold_in(own, 4), (count // 2,), 0, 1 << 20) % (slack + 1)
    tallies = tallies.at[donor].add(-shifted).at[receiver].add(shifted)
    members = jnp.searchsorted(jnp.cumsum(tallies), jnp.arange(rows * top), side="right").astype(jnp.int32)
    table = members.reshape(top, rows).T
    table = table[jax.random.permutation(jax.random.fold_in(own, 1), rows)]
    rotation = jax.random.randint(jax.random.fold_in(own, 2), (rows, 1), 0, top)
    return jnp.take_along_axis(table, (jnp.arange(top)[None, :] + rotation) % top, axis=1)


def portions_of(number_of, total, reach, skew, full):
    weights = [(1 << 20) // math.isqrt(grade ** skew) + 1 for grade in range(1, number_of + 1)]
    largest = reach if full else min(reach, max(-(-total // number_of), total * weights[0] // sum(weights)))
    least = 1 if total - largest >= number_of - 1 else 0
    counts, rest = [largest] + [least] * (number_of - 1), total - largest - least * (number_of - 1)
    while rest > 0:
        free = [i for i in range(1, number_of) if counts[i] < largest] or [i for i in range(1, number_of) if counts[i] < reach]
        pool, left = sum([weights[i] for i in free]), rest
        for i in free:
            more = min(reach - counts[i], max(1, left * weights[i] // pool), rest)
            counts[i] = counts[i] + more
            rest = rest - more
    return np.array(counts)


def gaussian(rng, dims, spread, bound, pieces=(), kind=jnp.bfloat16):
    values = jax.random.normal(rng, dims, jnp.float32) * spread
    if len(pieces) > 0:
        values = steps_of(rng, dims, pieces, -0.22, 0.18) * values
    return jnp.clip(values, min=-bound, max=bound).astype(kind)


def setup_inputs(seed: int = 0) -> dict:
    key_of = jax.random.split(jax.random.key(seed), 15)
    tokens = gaussian(key_of[0], (TOKENS, D), 1.0, 6.0, ((0, 8),))
    prev_logits = gaussian(key_of[1], (TOKENS, ALL_EXPERTS), 0.5, 3.0, ((0, 8),), jnp.float32)
    routes_keys = jax.random.split(jax.random.fold_in(key_of[2], 1), TOKENS // ROWS)
    routes_turns = jax.random.permutation(jax.random.fold_in(key_of[2], 3), TOKENS // ROWS)
    routes = jax.vmap(lambda own, number: deal_out(jax.random.fold_in(key_of[2], 2), own, number, ROWS, ALL_EXPERTS, 2, CAPACITY, 2))(routes_keys, routes_turns).reshape((TOKENS, 2))
    segments = draw_segments(jax.random.fold_in(key_of[14], 71), 0)
    gain_one = jnp.clip(1.0 + 0.1 * jax.random.normal(key_of[4], (D,), jnp.float32), 0.5, 1.5)
    w_qkv = gaussian(key_of[5], (D, 3, HEADS * HD), D ** -0.5, 0.21875, ((0, 2), (2, 4)), jnp.float32)
    w_out = gaussian(key_of[6], (HEADS * HD, D), (D // 16) ** -0.5, 0.875, ((0, 4), (1, 2)), jnp.float32)
    gain_two = jnp.clip(1.0 + 0.1 * jax.random.normal(key_of[7], (D,), jnp.float32), 0.5, 1.5)
    router = gaussian(key_of[8], (D, ALL_EXPERTS), (4 * D) ** -0.5, 0.109375, ((0, 2),), jnp.float32)
    const_proj = gaussian(key_of[9], (D, 4), D ** -0.5, 0.21875, ((0, 2),), jnp.float32)
    const_vec = gaussian(key_of[10], (2, D), 1.0, 6.0, ((1, 2),), jnp.float32)
    w_gate_up = gaussian(key_of[11], (EXPERTS, D, 2, FF), D ** -0.5, 0.21875, ((0, 4), (1, 2), (3, 4)), jnp.float32)
    w_down = gaussian(key_of[12], (EXPERTS, FF, D), (max(FF // 256, 1)) ** -0.5, 2.0, ((0, 4), (1, 4), (2, 2)), jnp.float32)
    cotangent = gaussian(key_of[13], (TOKENS, D), 1.0, 6.0, ((0, 8),))
    return {"tokens": tokens, "prev_logits": prev_logits, "routes": routes, "segments": segments, "gain_one": gain_one, "w_qkv": w_qkv, "w_out": w_out, "gain_two": gain_two, "router": router, "const_proj": const_proj, "const_vec": const_vec, "w_gate_up": w_gate_up, "w_down": w_down, "cotangent": cotangent}


EPS = 1e-06
NEG = -1e+30
HIGH = lax.Precision.HIGHEST

@jax.custom_vjp
def low(v):
    return lax.optimization_barrier(v.astype(jnp.bfloat16)).astype(jnp.float32)

@jax.custom_vjp
def low_back(v):
    return v

def low_keep(v):
    return (low(v), None)

def low_pass(kept, grad):
    return (grad,)

def back_keep(v):
    return (v, None)

def back_low(kept, grad):
    return (low(grad),)
low.defvjp(low_keep, low_pass)
low_back.defvjp(back_keep, back_low)

def norm_rows(values, gain):
    return values * lax.rsqrt(lax.optimization_barrier(jnp.mean(values * values, axis=-1, keepdims=True)) + EPS) * gain

def slot_tables(routes):
    flat_ids = routes.reshape(-1)
    entries = flat_ids.shape[0]
    one_hot = (flat_ids[:, None] == jnp.arange(EXPERTS, dtype=jnp.int32)[None, :]).astype(jnp.int32)
    places = lax.optimization_barrier(jnp.sum(one_hot * (jnp.cumsum(one_hot, axis=0) - 1), axis=1)).astype(jnp.int32)
    slot_ids = jnp.where(flat_ids < EXPERTS, flat_ids * CAPACITY + places, EXPERTS * CAPACITY).astype(jnp.int32)
    lookup = jnp.full((EXPERTS * CAPACITY + 1,), entries, jnp.int32)
    lookup = lookup.at[slot_ids].set(jnp.arange(entries, dtype=jnp.int32))
    return (slot_ids, lookup[:EXPERTS * CAPACITY])

def attend(queries, keys_in, values, segment_ids):
    total_len = queries.shape[0]
    scores = jnp.einsum('qhd,khd->hqk', queries, keys_in, precision=HIGH) * HD ** (-0.5)
    scores = low_back(scores)
    places = jnp.arange(total_len, dtype=jnp.int32)
    allowed = (places[None, :] <= places[:, None]) & (segment_ids[None, :] == segment_ids[:, None])
    scores = jnp.where(allowed[None], scores, NEG)
    weights = low(jax.nn.softmax(scores, axis=-1))
    return jnp.einsum('hqk,khd->qhd', weights, values, precision=HIGH)

def pick_rows(source, indices):
    return source[indices]

def reference(tokens, prev_logits, routes, segments, gain_one, w_qkv, w_out, gain_two, router, const_proj, const_vec, w_gate_up, w_down, cotangent):
    groups = N_DP * N_EXPERT
    row_count = SEQS * SEQ_LEN
    seq_total = groups * SEQS
    heads_part = HEADS // N_TENSOR
    width = heads_part * HD
    hidden = FF // N_TENSOR
    slot_ids, lookups = jax.vmap(slot_tables)(routes.reshape(groups, row_count, 2))
    kinds = (routes[:, :, None] == (EXPERTS + jnp.arange(4, dtype=jnp.int32))[None, None, :]).astype(jnp.float32)
    route_hot = (routes[:, :, None] == jnp.arange(ALL_EXPERTS, dtype=jnp.int32)[None, None, :]).astype(jnp.float32)
    seg_rows = segments.reshape(seq_total, SEQ_LEN)
    attend_saved = jax.checkpoint(attend)

    def one_sequence(packed):
        return attend_saved(packed[0], packed[1], packed[2], packed[3])

    def forward(inputs, gain_a, qkv_master, out_master, gain_b, router_master, mix_master, const_master, gate_up_master, down_master):
        gain_a = low(gain_a)
        qkv_weights = low(qkv_master)
        out_weights = low(out_master)
        gain_b = low(gain_b)
        route_weights = low(router_master)
        mix_weights = low(mix_master)
        const_rows = low(const_master)
        gate_up = low(gate_up_master)
        down_proj = low(down_master)
        normed_a = low(norm_rows(inputs, gain_a))
        attn_total = jnp.zeros_like(inputs)
        for group_idx in range(N_TENSOR):
            columns = qkv_weights[:, :, group_idx * width:(group_idx + 1) * width].reshape(D, 3 * width)
            projected = low_back(low(jnp.dot(low_back(normed_a), columns, precision=HIGH)))
            projected = projected.reshape(seq_total, SEQ_LEN, 3, heads_part, HD)
            attended = lax.map(one_sequence, (projected[:, :, 0], projected[:, :, 1], projected[:, :, 2], seg_rows))
            attended = low_back(low(attended.reshape(-1, width)))
            term = jnp.dot(attended, out_weights[group_idx * width:(group_idx + 1) * width], precision=HIGH)
            attn_total = attn_total + low_back(low(term))
        after_attn = inputs + attn_total
        normed_b = norm_rows(after_attn, gain_b)
        routed_low = low(normed_b)
        logits = low_back(jnp.dot(routed_low, route_weights, precision=HIGH)) + prev_logits
        chances = jax.nn.softmax(logits, axis=-1)
        gate_values = lax.optimization_barrier(jnp.sum(route_hot * chances[:, None, :], axis=-1))
        mixing = jax.nn.softmax(low_back(jnp.dot(routed_low, mix_weights, precision=HIGH)).reshape(-1, 2, 2), axis=-1)
        constants = mixing[:, :, 0:1] * normed_b[:, None, :] + mixing[:, :, 1:2] * const_rows[None, :, :]
        others = kinds[:, :, 1:2] * normed_b[:, None, :] + kinds[:, :, 2:3] * constants[:, None, 0, :] + kinds[:, :, 3:4] * constants[:, None, 1, :]
        padded = jnp.concatenate([routed_low.reshape(groups, row_count, D), jnp.zeros((groups, 1, D), jnp.float32)], axis=1)
        sent = low_back(jax.vmap(pick_rows)(padded, lookups // 2))
        sent = sent.reshape(groups, EXPERTS, CAPACITY, D)
        results = []
        for expert in range(EXPERTS):
            chosen = sent[:, expert].reshape(groups * CAPACITY, D)
            total = jnp.zeros_like(chosen)
            for group_idx in range(N_TENSOR):
                weights_part = gate_up[expert][:, :, group_idx * hidden:(group_idx + 1) * hidden].reshape(D, 2 * hidden)
                both = low_back(jnp.dot(low_back(chosen), weights_part, precision=HIGH))
                active = low(jax.nn.silu(both[:, :hidden]) * both[:, hidden:])
                total = total + low(jnp.dot(active, down_proj[expert, group_idx * hidden:(group_idx + 1) * hidden], precision=HIGH))
            results.append(low_back(low(total)).reshape(groups, CAPACITY, D))
        made = jnp.stack(results, axis=1).reshape(groups, EXPERTS * CAPACITY, D)
        made = jnp.concatenate([made, jnp.zeros((groups, 1, D), jnp.float32)], axis=1)
        picked = jax.vmap(pick_rows)(made, slot_ids).reshape(-1, 2, D)
        return after_attn + lax.optimization_barrier(jnp.sum(gate_values[:, :, None] * (picked + others), axis=1))
    primals = (tokens.astype(jnp.float32), gain_one, w_qkv, w_out, gain_two, router, const_proj, const_vec, w_gate_up, w_down)
    output, pullback = jax.vjp(forward, *primals)
    grads = pullback(cotangent.astype(jnp.float32))
    return (output, grads[0], grads[1], grads[2], grads[3], grads[4], grads[5], grads[6], grads[7], grads[8], grads[9])
```

```python
import functools
import jax
import jax.numpy as jnp
from jax import lax
from jax.experimental import pallas as pl
from jax.experimental.pallas import tpu as pltpu
from jax.sharding import PartitionSpec as P

D = 768
HD = 64
HEADS = 12
EXPERTS = 8
ALL_EXPERTS = 12
SEQ_LEN = 1024
CAPACITY = 480
DOC_BLOCK = 64
EPS = 1e-06
NEG = -1e30

LANES = 128
BLK = 256
WIN = BLK + 16
QBLOCKS = SEQ_LEN // BLK
PAIRS = HEADS // 2
NT = (((1,), (1,)), ((), ()))
TN = (((0,), (0,)), ((), ()))
F32 = jnp.float32
BF16 = jnp.bfloat16
MB = 1 << 20


def nn(a, b):
    return jnp.dot(a, b, preferred_element_type=F32)


def nt(a, b):
    return lax.dot_general(a, b, NT, preferred_element_type=F32)


def tn(a, b):
    return lax.dot_general(a, b, TN, preferred_element_type=F32)


def call(body, name, grid, in_specs, out_specs, out_shape, scratch=(), prefetch=0, flops=0, nbytes=0, vmem=48):
    return pl.pallas_call(
        body,
        name=name,
        out_shape=out_shape,
        grid_spec=pltpu.PrefetchScalarGridSpec(
            num_scalar_prefetch=prefetch,
            grid=grid,
            in_specs=in_specs,
            out_specs=out_specs,
            scratch_shapes=list(scratch),
        ),
        compiler_params=pltpu.CompilerParams(
            dimension_semantics=("arbitrary",) * len(grid), vmem_limit_bytes=vmem * MB
        ),
        cost_estimate=pl.CostEstimate(flops=flops, bytes_accessed=nbytes, transcendentals=0),
    )


def rows_spec(cols, rows=BLK):
    return pl.BlockSpec((rows, cols), lambda i, *_: (i, 0))


def full_spec(*shape):
    return pl.BlockSpec(shape, lambda *_: (0,) * len(shape))


def project_body(x_ref, gain_ref, w_ref, low_ref, out_ref):
    x = x_ref[...].astype(F32)
    factor = lax.rsqrt(jnp.mean(x * x, axis=-1, keepdims=True) + EPS)
    low = (x * factor * gain_ref[...]).astype(BF16)
    low_ref[...] = low
    out_ref[...] = nn(low, w_ref[...]).astype(BF16)


def project(tokens, gain, weights):
    rows = tokens.shape[0]
    cols = weights.shape[1]
    return call(
        project_body,
        "norm_project",
        (rows // BLK,),
        [rows_spec(D), full_spec(1, D), full_spec(D, cols)],
        [rows_spec(D), rows_spec(cols)],
        [jax.ShapeDtypeStruct((rows, D), BF16), jax.ShapeDtypeStruct((rows, cols), BF16)],
        flops=2 * rows * D * cols,
        nbytes=rows * (D + D + cols) * 2 + D * cols * 2,
    )(tokens, gain, weights)


def split_heads(v):
    first = lax.broadcasted_iota(jnp.int32, v.shape, 1) < HD
    zero = jnp.zeros_like(v)
    return (jnp.where(first, v, zero), jnp.where(first, zero, v))


def pair_mask(key_block, query_block, starts, diagonal):
    key_at = lax.broadcasted_iota(jnp.int32, (BLK, BLK), 0)
    mask = key_at >= starts - key_block * BLK
    if diagonal:
        mask = mask & (key_at <= lax.broadcasted_iota(jnp.int32, (BLK, BLK), 1))
    return mask


def attend_body(low_ref, q_ref, k_ref, v_ref, start_ref, o_ref, lse_ref, vt_ref):
    seq = pl.program_id(0)
    for kb in range(QBLOCKS):
        vt_ref[kb] = v_ref[kb * BLK : (kb + 1) * BLK, :].T
    for qb in range(QBLOCKS):
        here = slice(qb * BLK, (qb + 1) * BLK)
        queries = split_heads(q_ref[here, :] * jnp.asarray(HD**-0.5, BF16))
        starts = start_ref[0, :, here]

        def step(kb, carry, diagonal):
            keys = k_ref[pl.ds(pl.multiple_of(kb * BLK, BLK), BLK), :]
            mask = pair_mask(kb, qb, starts, diagonal)
            out = []
            for h in range(2):
                highest, total, acc = carry[3 * h : 3 * h + 3]
                scores = jnp.where(mask, nt(keys, queries[h]), NEG)
                now = jnp.maximum(highest, jnp.max(scores, axis=0, keepdims=True))
                weights = jnp.exp(scores - now)
                fade = jnp.exp(highest - now)
                total = total * fade + jnp.sum(weights, axis=0, keepdims=True)
                acc = acc * fade + nn(vt_ref[kb, h * HD : (h + 1) * HD, :], weights.astype(BF16))
                out += [now, total, acc]
            return tuple(out)

        empty = (jnp.full((1, BLK), NEG, F32), jnp.zeros((1, BLK), F32), jnp.zeros((HD, BLK), F32))
        carry = step(qb, empty + empty, True)
        if qb > 0:
            carry = lax.fori_loop(
                low_ref[seq * QBLOCKS + qb], qb, lambda kb, c: step(kb, c, False), carry
            )
        both = jnp.concatenate([carry[2] / carry[1], carry[5] / carry[4]], axis=0)
        o_ref[here, :] = both.T.astype(BF16)
        lse_ref[0, 0, 0:1, here] = carry[0] + jnp.log(carry[1])
        lse_ref[0, 0, 1:2, here] = carry[3] + jnp.log(carry[4])


def head_spec(offset):
    return pl.BlockSpec((SEQ_LEN, 2 * HD), lambda s, p, *_: (s, p + offset))


def attend(qkv, starts, lowest):
    rows = qkv.shape[0]
    seqs = rows // SEQ_LEN
    return call(
        attend_body,
        "attend",
        (seqs, PAIRS),
        [
            head_spec(0),
            head_spec(PAIRS),
            head_spec(2 * PAIRS),
            pl.BlockSpec((1, 1, SEQ_LEN), lambda s, p, *_: (s, 0, 0)),
        ],
        [head_spec(0), pl.BlockSpec((1, 1, 2, SEQ_LEN), lambda s, p, *_: (s, p, 0, 0))],
        [
            jax.ShapeDtypeStruct((rows, D), BF16),
            jax.ShapeDtypeStruct((seqs, PAIRS, 2, SEQ_LEN), F32),
        ],
        scratch=[pltpu.VMEM((QBLOCKS, 2 * HD, BLK), BF16)],
        prefetch=1,
        flops=4 * rows * SEQ_LEN * D,
        nbytes=rows * D * 8,
    )(lowest, qkv, qkv, qkv, starts)


def attend_back_body(low_ref, q_ref, k_ref, v_ref, start_ref, do_ref, o_ref, lse_ref, g_ref, kt_ref, dk_ref, dv_ref):
    seq = pl.program_id(0)
    pick = (
        lax.broadcasted_iota(jnp.int32, (8, 2 * HD), 1) // HD
        == lax.broadcasted_iota(jnp.int32, (8, 2 * HD), 0)
    ).astype(F32)
    for kb in range(QBLOCKS):
        kt_ref[kb] = k_ref[kb * BLK : (kb + 1) * BLK, :].T
    for qb in range(QBLOCKS):
        here = slice(qb * BLK, (qb + 1) * BLK)
        queries = split_heads(q_ref[here, :] * jnp.asarray(HD**-0.5, BF16))
        upstream = do_ref[here, :]
        ups = split_heads(upstream)
        deltas = lax.dot_general(
            pick,
            upstream.astype(F32) * o_ref[here, :].astype(F32),
            NT,
            precision=lax.Precision.HIGHEST,
            preferred_element_type=F32,
        )
        starts = start_ref[0, :, here]

        def step(kb, carry, diagonal):
            at = pl.ds(pl.multiple_of(kb * BLK, BLK), BLK)
            keys = k_ref[at, :]
            values = v_ref[at, :]
            mask = pair_mask(kb, qb, starts, diagonal)
            out = []
            dk = dv = None
            for h in range(2):
                scores = jnp.where(mask, nt(keys, queries[h]), NEG)
                weights = jnp.exp(scores - lse_ref[0, 0, h : h + 1, here])
                slopes = (weights * (nt(values, ups[h]) - deltas[h : h + 1, :])).astype(BF16)
                dv_h = nn(weights.astype(BF16), ups[h])
                dk_h = nn(slopes, queries[h])
                dv = dv_h if dv is None else dv + dv_h
                dk = dk_h if dk is None else dk + dk_h
                out.append(carry[h] + nn(kt_ref[kb, h * HD : (h + 1) * HD, :], slopes))
            if diagonal:
                dk_ref[at, :] = dk
                dv_ref[at, :] = dv
            else:
                dk_ref[at, :] += dk
                dv_ref[at, :] += dv
            return tuple(out)

        zero = jnp.zeros((HD, BLK), F32)
        carry = step(qb, (zero, zero), True)
        if qb > 0:
            carry = lax.fori_loop(
                low_ref[seq * QBLOCKS + qb], qb, lambda kb, c: step(kb, c, False), carry
            )
        both = jnp.concatenate(carry, axis=0) * (HD**-0.5)
        g_ref[0, here, :] = both.T.astype(BF16)
    g_ref[1] = dk_ref[...].astype(BF16)
    g_ref[2] = dv_ref[...].astype(BF16)


def attend_back(qkv, starts, lowest, grad_out, attended, log_sums):
    rows = qkv.shape[0]
    seqs = rows // SEQ_LEN
    return call(
        attend_back_body,
        "attend_back",
        (seqs, PAIRS),
        [
            head_spec(0),
            head_spec(PAIRS),
            head_spec(2 * PAIRS),
            pl.BlockSpec((1, 1, SEQ_LEN), lambda s, p, *_: (s, 0, 0)),
            head_spec(0),
            head_spec(0),
            pl.BlockSpec((1, 1, 2, SEQ_LEN), lambda s, p, *_: (s, p, 0, 0)),
        ],
        pl.BlockSpec((3, SEQ_LEN, 2 * HD), lambda s, p, *_: (0, s, p)),
        jax.ShapeDtypeStruct((3, rows, D), BF16),
        scratch=[
            pltpu.VMEM((QBLOCKS, 2 * HD, BLK), BF16),
            pltpu.VMEM((SEQ_LEN, 2 * HD), F32),
            pltpu.VMEM((SEQ_LEN, 2 * HD), F32),
        ],
        prefetch=1,
        flops=10 * rows * SEQ_LEN * D,
        nbytes=rows * D * 16,
    )(lowest, qkv, qkv, qkv, starts, grad_out, attended, log_sums)


def lane_of(shape):
    return lax.broadcasted_iota(jnp.int32, shape, 1)


def members_of(routes):
    lane = lane_of((routes.shape[0], LANES))
    return ((lane == routes[:, 0:1]) | (lane == routes[:, 1:2])).astype(F32)


def middle_body(att_ref, w_ref, x_ref, gain_ref, rw_ref, cv_ref, cot_ref, prev_ref, after_ref, low_ref, info_ref):
    after = x_ref[...].astype(F32) + nn(att_ref[...], w_ref[...])
    after_ref[...] = after
    factor = lax.rsqrt(jnp.mean(after * after, axis=-1, keepdims=True) + EPS)
    normed = after * factor * gain_ref[...]
    low = normed.astype(BF16)
    low_ref[...] = low
    products = nt(low, rw_ref[...])
    mine, swapped = products[:, :LANES], products[:, LANES:]
    cot = cot_ref[...]
    dots = nt(cot, cv_ref[...])
    dot_normed = jnp.sum(cot.astype(F32) * normed, axis=-1, keepdims=True)
    lane = lane_of(mine.shape)
    logits = jnp.where(lane < ALL_EXPERTS, mine + prev_ref[...], NEG)
    grown = jnp.exp(logits - jnp.max(logits, axis=-1, keepdims=True))
    chances = grown / jnp.sum(grown, axis=-1, keepdims=True)
    mixing = 1.0 / (1.0 + jnp.exp(swapped - mine))
    info = jnp.where(lane < 12, chances, jnp.where(lane < 16, mixing, dots))
    info_ref[...] = jnp.where(lane == 18, dot_normed, info)


def middle(attended, w_out, tokens, gain, rw, cv, cot, prev):
    rows = tokens.shape[0]
    return call(
        middle_body,
        "out_norm_route",
        (rows // BLK,),
        [
            rows_spec(D),
            full_spec(D, D),
            rows_spec(D),
            full_spec(1, D),
            full_spec(2 * LANES, D),
            full_spec(LANES, D),
            rows_spec(D),
            rows_spec(LANES),
        ],
        [rows_spec(D), rows_spec(D), rows_spec(LANES)],
        [
            jax.ShapeDtypeStruct((rows, D), F32),
            jax.ShapeDtypeStruct((rows, D), BF16),
            jax.ShapeDtypeStruct((rows, LANES), F32),
        ],
        flops=2 * rows * D * (D + 3 * LANES),
        nbytes=rows * D * 12 + rows * LANES * 8,
    )(attended, w_out, tokens, gain, rw, cv, cot, prev)


def dispatch_body(start_ref, rows_ref, rank_ref, out_ref, acc_ref):
    expert = pl.program_id(0)
    acc_ref[...] = jnp.zeros_like(acc_ref)
    blocks = rows_ref.shape[0] // BLK
    for tb in range(blocks):
        here = slice(tb * BLK, (tb + 1) * BLK)
        first = pl.multiple_of(start_ref[expert * blocks + tb] // 16 * 16, 16)
        slot = lax.broadcasted_iota(jnp.int32, (WIN, BLK), 0)
        chosen = jnp.where(rank_ref[0, :, here] - first == slot, 1.0, 0.0).astype(BF16)
        acc_ref[pl.ds(first, WIN), :] += nn(chosen, rows_ref[here, :]).astype(acc_ref.dtype)
    out_ref[0] = acc_ref[:CAPACITY, :]


def dispatch(rows, ranks, starts, dtype, name):
    count, cols = rows.shape
    experts = ranks.shape[0]
    return call(
        dispatch_body,
        name,
        (experts,),
        [full_spec(count, cols), pl.BlockSpec((1, 1, count), lambda e, *_: (e, 0, 0))],
        pl.BlockSpec((1, CAPACITY, cols), lambda e, *_: (e, 0, 0)),
        jax.ShapeDtypeStruct((experts, CAPACITY, cols), dtype),
        scratch=[pltpu.VMEM((CAPACITY + WIN, cols), dtype)],
        prefetch=1,
        flops=2 * experts * count * WIN * cols,
        nbytes=(count + experts * CAPACITY) * cols * 2,
    )(starts, rows, ranks)


def combine_body(start_ref, first_ref, second_ref, rank_ref, info_ref, *rest, blocks):
    if len(rest) == 1:
        (out_ref,) = rest
        dg_ref = None
    else:
        dg_ref, out_ref, pick_ref = rest
    tb = pl.program_id(0)
    ranks = rank_ref[...]
    info = info_ref[...]
    slot = lax.broadcasted_iota(jnp.int32, (BLK, WIN), 1)
    lane = lane_of((BLK, LANES))
    acc = jnp.zeros((BLK, D), F32)
    picked = jnp.zeros((BLK, LANES), F32)
    for expert in range(EXPERTS):
        rows_ref = (first_ref, second_ref)[expert % 2]
        first = jnp.minimum(start_ref[expert * blocks + tb] // 16 * 16, CAPACITY - WIN)
        first = pl.multiple_of(first, 16)
        chosen = jnp.where(ranks[:, expert : expert + 1] - first == slot, 1.0, 0.0).astype(BF16)
        acc += info[:, expert : expert + 1] * nn(chosen, rows_ref[expert // 2, pl.ds(first, WIN), :])
        if dg_ref is not None:
            mine = (lane % 16 == expert) & (lane < 48)
            picked += jnp.where(mine, nn(chosen, dg_ref[pl.ds(first, WIN), :]), 0.0)
    out_ref[...] = acc.astype(BF16)
    if dg_ref is not None:
        pick_ref[...] = picked + pltpu.roll(picked, LANES - 16, 1) + pltpu.roll(picked, LANES - 32, 1)


def combine(first, second, rank_cols, info, starts, dg, name):
    count = rank_cols.shape[0]
    blocks = count // BLK
    owners = first.shape[0]
    extra = [] if dg is None else [dg]
    outs = [jax.ShapeDtypeStruct((count, D), BF16)]
    out_specs = [rows_spec(D)]
    if dg is not None:
        outs.append(jax.ShapeDtypeStruct((count, LANES), F32))
        out_specs.append(rows_spec(LANES))
    return call(
        functools.partial(combine_body, blocks=blocks),
        name,
        (blocks,),
        [
            full_spec(owners, CAPACITY, D),
            full_spec(owners, CAPACITY, D),
            rows_spec(LANES),
            rows_spec(LANES),
        ]
        + [full_spec(CAPACITY, LANES)] * len(extra),
        out_specs,
        outs,
        prefetch=1,
        flops=2 * EXPERTS * count * WIN * D,
        nbytes=(count + EXPERTS * CAPACITY) * D * 2,
    )(starts, first, second, rank_cols, info, *extra)


def expert_body(x_ref, c_ref, gu_ref, dn_ref, act_ref, both_ref, dx_ref, dg_ref):
    hidden = dn_ref.shape[0]
    both = nn(x_ref[0], gu_ref[...])
    gate, up = both[:, :hidden], both[:, hidden:]
    sig = jax.nn.sigmoid(gate)
    act = (gate * sig * up).astype(BF16)
    act_ref[0] = act
    grad_act = nt(c_ref[0], dn_ref[...])
    dg_ref[0] = jnp.sum(act.astype(F32) * grad_act, axis=-1, keepdims=True)
    grad_gate = grad_act * up * sig * (1.0 + gate * (1.0 - sig))
    grad_up = grad_act * (gate * sig)
    grad_both = jnp.concatenate([grad_gate, grad_up], axis=-1).astype(BF16)
    both_ref[0] = grad_both
    dx_ref[0] = nt(grad_both, gu_ref[...]).astype(BF16)


def expert_core(x, cot, gate_up, down):
    sources = x.shape[0]
    hidden = down.shape[0]

    def block(cols):
        return pl.BlockSpec((1, CAPACITY, cols), lambda s: (s, 0, 0))

    return call(
        expert_body,
        "expert",
        (sources,),
        [block(D), block(D), full_spec(D, 2 * hidden), full_spec(hidden, D)],
        [block(hidden), block(2 * hidden), block(D), block(1)],
        [
            jax.ShapeDtypeStruct((sources, CAPACITY, hidden), BF16),
            jax.ShapeDtypeStruct((sources, CAPACITY, 2 * hidden), BF16),
            jax.ShapeDtypeStruct((sources, CAPACITY, D), BF16),
            jax.ShapeDtypeStruct((sources, CAPACITY, 1), F32),
        ],
        flops=2 * sources * CAPACITY * D * hidden * 5,
        nbytes=sources * CAPACITY * (3 * D + 3 * hidden) * 2 + 3 * D * hidden * 2,
    )(x, cot, gate_up, down)


def output_body(after_ref, moe_ref, info_ref, routes_ref, gain_ref, cv_ref, out_ref):
    after = after_ref[...]
    factor = lax.rsqrt(jnp.mean(after * after, axis=-1, keepdims=True) + EPS)
    info = info_ref[...]
    gates = info * members_of(routes_ref[...])
    coef = gates[:, 9:10] + gates[:, 10:11] * info[:, 12:13] + gates[:, 11:12] * info[:, 14:15]
    out = after * (1.0 + coef * factor * gain_ref[...]) + moe_ref[...].astype(F32)
    out = out + (gates[:, 10:11] * info[:, 13:14]) * cv_ref[0:1, :]
    out_ref[...] = out + (gates[:, 11:12] * info[:, 15:16]) * cv_ref[1:2, :]


def finish_output(after, moe, info, routes, gain, cv):
    rows = after.shape[0]
    return call(
        output_body,
        "output",
        (rows // BLK,),
        [rows_spec(D), rows_spec(D), rows_spec(LANES), rows_spec(2), full_spec(1, D), full_spec(2, D)],
        rows_spec(D),
        jax.ShapeDtypeStruct((rows, D), F32),
        nbytes=rows * D * 10,
    )(after, moe, info, routes, gain, cv)


def back_body(after_ref, cot_ref, moe_ref, info_ref, dg_ref, routes_ref, gain_ref, rw_ref, low_ref, w_ref, grad_ref, glow_ref, datt_ref, small_ref):
    after = after_ref[...]
    factor = lax.rsqrt(jnp.mean(after * after, axis=-1, keepdims=True) + EPS)
    xhat = after * factor
    gain = gain_ref[...]
    cot = cot_ref[...].astype(F32)
    info = info_ref[...]
    members = members_of(routes_ref[...])
    gates = info * members
    lane = lane_of(info.shape)
    dot_normed = info[:, 18:19]

    grad = jnp.where(lane < EXPERTS, dg_ref[...], 0.0)
    grad = grad + jnp.where(lane == 9, dot_normed, 0.0)
    grad_mix = jnp.zeros_like(grad)
    coef = gates[:, 9:10]
    spare = []
    for c in range(2):
        first, second = info[:, 12 + 2 * c : 13 + 2 * c], info[:, 13 + 2 * c : 14 + 2 * c]
        dot_const = info[:, 16 + c : 17 + c]
        weight = gates[:, 10 + c : 11 + c]
        inner = first * dot_normed + second * dot_const
        grad = grad + jnp.where(lane == 10 + c, inner, 0.0)
        grad_mix = grad_mix + jnp.where(lane == 12 + 2 * c, first * weight * (dot_normed - inner), 0.0)
        grad_mix = grad_mix + jnp.where(lane == 13 + 2 * c, second * weight * (dot_const - inner), 0.0)
        coef = coef + weight * first
        spare.append(weight * second)
    grad = grad * members
    chances = jnp.where(lane < ALL_EXPERTS, info, 0.0)
    grad_logits = chances * (grad - jnp.sum(chances * grad, axis=-1, keepdims=True))
    slopes = (grad_logits + grad_mix).astype(BF16)

    grad_normed = coef * cot + nn(slopes, rw_ref[...]) + moe_ref[...].astype(F32)
    weighted = grad_normed * gain
    inner = jnp.mean(weighted * xhat, axis=-1, keepdims=True)
    grad_after = cot + factor * (weighted - xhat * inner)
    grad_ref[...] = grad_after
    low = grad_after.astype(BF16)
    glow_ref[...] = low
    datt_ref[...] = nt(low, w_ref[...]).astype(BF16)

    @pl.when(pl.program_id(0) == 0)
    def _():
        small_ref[...] = jnp.zeros_like(small_ref)

    small_ref[0:16, :] += tn(slopes, low_ref[...])[:16, :]
    small_ref[16:17, :] += jnp.sum(grad_normed * xhat, axis=0, keepdims=True)
    small_ref[17:18, :] += jnp.sum(spare[0] * cot, axis=0, keepdims=True)
    small_ref[18:19, :] += jnp.sum(spare[1] * cot, axis=0, keepdims=True)


def back(after, cot, moe, info, dg, routes, gain, rw, low, w_out):
    rows = after.shape[0]
    return call(
        back_body,
        "route_norm_back",
        (rows // BLK,),
        [
            rows_spec(D),
            rows_spec(D),
            rows_spec(D),
            rows_spec(LANES),
            rows_spec(LANES),
            rows_spec(2),
            full_spec(1, D),
            full_spec(LANES, D),
            rows_spec(D),
            full_spec(D, D),
        ],
        [rows_spec(D), rows_spec(D), rows_spec(D), full_spec(24, D)],
        [
            jax.ShapeDtypeStruct((rows, D), F32),
            jax.ShapeDtypeStruct((rows, D), BF16),
            jax.ShapeDtypeStruct((rows, D), BF16),
            jax.ShapeDtypeStruct((24, D), F32),
        ],
        flops=2 * rows * D * (D + 2 * LANES),
        nbytes=rows * D * 18,
    )(after, cot, moe, info, dg, routes, gain, rw, low, w_out)


def final_body(g_ref, w_ref, x_ref, gain_ref, after_ref, out_ref, small_ref):
    grad = nt(g_ref[0], w_ref[:, :D]) + nt(g_ref[1], w_ref[:, D : 2 * D]) + nt(g_ref[2], w_ref[:, 2 * D :])
    x = x_ref[...].astype(F32)
    factor = lax.rsqrt(jnp.mean(x * x, axis=-1, keepdims=True) + EPS)
    xhat = x * factor
    weighted = grad * gain_ref[...]
    inner = jnp.mean(weighted * xhat, axis=-1, keepdims=True)
    out_ref[...] = after_ref[...] + factor * (weighted - xhat * inner)

    @pl.when(pl.program_id(0) == 0)
    def _():
        small_ref[...] = jnp.zeros_like(small_ref)

    small_ref[0:1, :] += jnp.sum(grad * xhat, axis=0, keepdims=True)


def final(grads, weights, tokens, gain, grad_after):
    rows = tokens.shape[0]
    return call(
        final_body,
        "norm_back",
        (rows // BLK,),
        [
            pl.BlockSpec((3, BLK, D), lambda i: (0, i, 0)),
            full_spec(D, 3 * D),
            rows_spec(D),
            full_spec(1, D),
            rows_spec(D),
        ],
        [rows_spec(D), full_spec(8, D)],
        [jax.ShapeDtypeStruct((rows, D), F32), jax.ShapeDtypeStruct((8, D), F32)],
        flops=6 * rows * D * D,
        nbytes=rows * D * 16,
    )(grads, weights, tokens, gain, grad_after)


def gather_dp(x, axis):
    n = lax.axis_size("dp")
    if n != 2:
        return lax.all_gather(x, "dp", axis=axis, tiled=True)
    other = lax.ppermute(x, "dp", [(0, 1), (1, 0)])
    here = lax.axis_index("dp") == 0
    return jnp.concatenate([jnp.where(here, x, other), jnp.where(here, other, x)], axis=axis)


def scatter_dp(x, axis):
    n = lax.axis_size("dp")
    if n != 2:
        return lax.psum_scatter(x.astype(BF16), "dp", scatter_dimension=axis, tiled=True).astype(F32)
    half = x.shape[axis] // 2
    me = lax.axis_index("dp")
    keep = lax.dynamic_slice_in_dim(x, me * half, half, axis)
    send = lax.dynamic_slice_in_dim(x, (1 - me) * half, half, axis).astype(BF16)
    return keep.astype(F32) + lax.ppermute(send, "dp", [(0, 1), (1, 0)]).astype(F32)


def sum_over(x, axis_name):
    n = lax.axis_size(axis_name)
    if n & (n - 1):
        return lax.psum(x.astype(BF16), axis_name).astype(F32)
    step = 1
    while step < n:
        low = x.astype(BF16)
        other = lax.ppermute(low, axis_name, [(i, i ^ step) for i in range(n)])
        x = low.astype(F32) + other.astype(F32)
        step *= 2
    return x


def gather_groups(x):
    n = lax.axis_size("tensor")
    me = lax.axis_index("tensor")
    parts = [x] + [
        lax.ppermute(x, "tensor", [(i, (i + k) % n) for i in range(n)]) for k in range(1, n)
    ]
    stacked = jnp.stack(parts)
    return jnp.take(stacked, (me - jnp.arange(n)) % n, axis=0)


def sum_tensor(x, pieces):
    n = lax.axis_size("tensor")
    if n != 4:
        return lax.psum(x, "tensor")
    me = lax.axis_index("tensor")
    outer = (me == 0) | (me == n - 1)
    size = x.shape[0] // pieces
    done = []
    for c in range(pieces):
        part = x[c * size : (c + 1) * size]
        other = lax.ppermute(part, "tensor", [(0, 1), (3, 2)])
        part = (part.astype(F32) + other.astype(F32)).astype(BF16)
        other = lax.ppermute(part, "tensor", [(1, 2), (2, 1)])
        part = (part.astype(F32) + other.astype(F32)).astype(BF16)
        other = lax.ppermute(part, "tensor", [(1, 0), (2, 3)])
        done.append(jnp.where(outer, other, part))
    return jnp.concatenate(done, axis=0)


def exchange(x):
    return lax.all_to_all(x, "expert", split_axis=0, concat_axis=0, tiled=True)


def route_tables(routes):
    count = routes.shape[0]
    blocks = count // BLK
    ids = jnp.arange(EXPERTS, dtype=jnp.int32)[:, None]
    member = (routes[:, 0][None, :] == ids) | (routes[:, 1][None, :] == ids)
    ones = member.astype(BF16).reshape(EXPERTS, blocks, BLK)
    earlier = (jnp.arange(BLK)[:, None] < jnp.arange(BLK)[None, :]).astype(BF16)
    inside = jnp.einsum("ebt,tu->ebu", ones, earlier, preferred_element_type=F32)
    counts = jnp.sum(ones.astype(F32), axis=-1)
    starts = jnp.cumsum(counts, axis=1) - counts
    ranks = (inside + starts[:, :, None]).astype(jnp.int32).reshape(EXPERTS, count)
    ranks = jnp.where(member, ranks, -(1 << 20))
    return (ranks, starts.astype(jnp.int32))


def document_tables(segments):
    seqs = segments.shape[0] // SEQ_LEN
    marks = segments.reshape(seqs, SEQ_LEN // DOC_BLOCK, DOC_BLOCK)[:, :, 0]
    begin = DOC_BLOCK * jnp.sum((marks[:, None, :] < marks[:, :, None]).astype(jnp.int32), axis=-1)
    starts = jnp.broadcast_to(begin[:, :, None], begin.shape + (DOC_BLOCK,)).reshape(seqs, 1, SEQ_LEN)
    lowest = begin[:, :: BLK // DOC_BLOCK] // BLK
    return (starts, lowest.reshape(-1))


def three_parts(x):
    high = x.astype(BF16)
    rest = x - high.astype(F32)
    mid = rest.astype(BF16)
    return (high, mid, (rest - mid.astype(F32)).astype(BF16))


def on_device(
    tokens,
    prev_logits,
    routes,
    segments,
    gain_one,
    w_qkv,
    w_out,
    gain_two,
    router,
    const_proj,
    const_vec,
    w_gate_up,
    w_down,
    cotangent,
):
    rows = tokens.shape[0]
    owners = lax.axis_size("expert")
    groups = lax.axis_size("tensor")
    group = lax.axis_index("tensor")
    local_experts = EXPERTS // owners
    width = w_out.shape[0]
    slice_rows = w_qkv.shape[0]

    in_mine = gather_groups(w_qkv.astype(BF16).reshape(slice_rows, 3 * width))
    in_mine = in_mine.reshape(groups, slice_rows, 3, width).transpose(1, 2, 0, 3)
    in_all = gather_dp(in_mine.reshape(slice_rows, 3 * D), 0)
    out_mine = gather_groups(w_out.astype(BF16)).reshape(D, slice_rows)
    out_all = gather_dp(out_mine, 1)
    small = jnp.concatenate(
        [router.T, const_proj.T, gain_one[None], gain_two[None], const_vec], axis=0
    ).astype(BF16)
    small = gather_dp(small, 1)
    gain_a = small[16:17].astype(F32)
    gain_b = small[17:18].astype(F32)
    const_rows = small[18:20].astype(F32)
    mains = jnp.pad(small[:16], ((0, LANES - 16), (0, 0)))
    swaps = jnp.stack([small[13], small[12], small[15], small[14]])
    routing = jnp.concatenate([mains, jnp.pad(swaps, ((12, LANES - 16), (0, 0)))], axis=0)
    const_low = jnp.pad(small[18:20], ((16, LANES - 18), (0, 0)))

    ranks, block_starts = route_tables(routes)
    rank_cols = jnp.pad(ranks.T, ((0, 0), (0, LANES - EXPERTS)))
    per_expert = ranks.reshape(owners, local_experts, 1, rows)
    per_start = block_starts.reshape(owners, local_experts, -1)
    table = [
        (per_expert[:, j], per_start[:, j].reshape(-1)) for j in range(local_experts)
    ]
    cot_in = [
        exchange(dispatch(cotangent, r, s, BF16, "send_cot")) for r, s in table
    ]
    all_starts = block_starts.reshape(-1)

    hidden = w_down.shape[1]
    gate_up = gather_dp(w_gate_up.astype(BF16).reshape(local_experts, slice_rows, 2 * hidden), 1)
    down = gather_dp(w_down.astype(BF16), 2)

    starts, lowest = document_tables(segments)
    normed_low, qkv = project(tokens, gain_a, in_all)
    attended, log_sums = attend(qkv, starts, lowest)
    prev = jnp.pad(prev_logits, ((0, 0), (0, LANES - ALL_EXPERTS)))
    after_attn, routed_low, info = middle(
        attended, out_all, tokens, gain_b, routing, const_low, cotangent, prev
    )

    rows_in = [exchange(dispatch(routed_low, r, s, BF16, "send_rows")) for r, s in table]
    acts, boths, back_rows, back_dots = [], [], [], []
    for j in range(local_experts):
        act, both, grad_rows, dots = expert_core(rows_in[j], cot_in[j], gate_up[j], down[j])
        acts.append(act)
        boths.append(both)
        back_rows.append(exchange(grad_rows))
        back_dots.append(dots.reshape(owners, CAPACITY))
    dots = exchange(jnp.stack(back_dots, axis=1)).reshape(EXPERTS, CAPACITY)
    dots = jnp.concatenate(
        [jnp.pad(p, ((0, 8), (0, 0))) for p in three_parts(dots)], axis=0
    )
    dots = jnp.pad(dots.T, ((0, 0), (0, LANES - 48)))
    grad_part, dots_part = combine(
        back_rows[0], back_rows[1], rank_cols, info, all_starts, dots, "combine_grads"
    )
    grad_moe = sum_tensor(grad_part, 4)
    dot_sums = lax.psum(dots_part[:, :EXPERTS].T, "tensor").T
    dot_sums = jnp.pad(dot_sums, ((0, 0), (0, LANES - EXPERTS)))

    outs_back = [
        exchange(
            jnp.einsum("scf,fd->scd", acts[j], down[j], preferred_element_type=F32).astype(BF16)
        )
        for j in range(local_experts)
    ]
    (out_part,) = combine(
        outs_back[0], outs_back[1], rank_cols, info, all_starts, None, "combine_out"
    )
    output = finish_output(
        after_attn, sum_tensor(out_part, 4), info, routes, gain_b, const_rows
    )

    grad_after, grad_low, grad_att, small_grads = back(
        after_attn, cotangent, grad_moe, info, dot_sums, routes, gain_b, mains, routed_low, out_all
    )
    grad_qkv = attend_back(qkv, starts, lowest, grad_att, attended, log_sums)
    grad_tokens, gain_grads = final(grad_qkv, in_all, tokens, gain_a, grad_after)

    chance_parts = jnp.concatenate(
        [jnp.pad(p, ((0, 0), (0, 8))) for p in three_parts(info[:, :EXPERTS])], axis=1
    )
    chance_parts = jnp.pad(chance_parts, ((0, 0), (0, LANES - 48)))
    grad_gate_up, grad_down = [], []
    for j in range(local_experts):
        sent = dispatch(chance_parts, *table[j], F32, "send_gates")
        ids = local_experts * jnp.arange(owners)[:, None] + j
        mine = (jnp.arange(LANES)[None, :] % 16 == ids) & (jnp.arange(LANES)[None, :] < 48)
        gates = exchange(jnp.sum(jnp.where(mine[:, None, :], sent, 0.0), axis=-1))
        gated = (gates[:, :, None] * boths[j].astype(F32)).astype(BF16)
        gated_cot = (gates[:, :, None] * cot_in[j].astype(F32)).astype(BF16)
        grad_gate_up.append(
            jnp.einsum("scd,scf->df", rows_in[j], gated, preferred_element_type=F32)
        )
        grad_down.append(
            jnp.einsum("scf,scd->fd", acts[j], gated_cot, preferred_element_type=F32)
        )
    grad_gate_up = scatter_dp(jnp.stack(grad_gate_up), 1).reshape(w_gate_up.shape)
    grad_down = scatter_dp(jnp.stack(grad_down), 2)

    own = lax.dynamic_slice_in_dim(grad_qkv, group * width, width, 2)
    grad_in_w = jnp.einsum("td,ctm->dcm", normed_low, own, preferred_element_type=F32)
    grad_in_w = sum_over(scatter_dp(grad_in_w.reshape(D, 3 * width), 0), "expert")
    own_att = lax.dynamic_slice_in_dim(attended, group * width, width, 1)
    grad_out_w = jnp.einsum("tm,td->md", own_att, grad_low, preferred_element_type=F32)
    grad_out_w = sum_over(scatter_dp(grad_out_w, 1), "expert")
    small_grads = sum_over(scatter_dp(small_grads, 1), "expert")
    gain_grads = sum_over(scatter_dp(gain_grads, 1), "expert")
    return (
        output,
        grad_tokens,
        gain_grads[0],
        grad_in_w.reshape(w_qkv.shape),
        grad_out_w,
        small_grads[16],
        small_grads[:12].T,
        small_grads[12:16].T,
        small_grads[17:19],
        grad_gate_up,
        grad_down,
    )


def solution(mesh):
    token_spec = P(("dp", "expert"), None)
    weight_specs = (
        P("dp"),
        P("dp", None, "tensor"),
        P("tensor", "dp"),
        P("dp"),
        P("dp", None),
        P("dp", None),
        P(None, "dp"),
        P("expert", "dp", None, "tensor"),
        P("expert", "tensor", "dp"),
    )
    return jax.shard_map(
        on_device,
        mesh=mesh,
        in_specs=(token_spec, token_spec, token_spec, P(("dp", "expert"))) + weight_specs + (token_spec,),
        out_specs=(token_spec, token_spec) + weight_specs,
        check_vma=False,
    )
```

```python
import functools
import jax
import jax.numpy as jnp
from jax import lax
from jax.experimental import pallas as pl
from jax.experimental.pallas import tpu as pltpu
from jax.sharding import PartitionSpec as P

D = 768
HD = 64
EXPERTS = 8
ALL_EXPERTS = 12
SEQ_LEN = 1024
CAPACITY = 480
DOC_BLOCK = 64
EPS = 1e-06
NEG = -1e30

LANES = 128
BLK = 256
SENT = CAPACITY + 16
WIN = BLK + 16
QBLOCKS = SEQ_LEN // BLK
CHUNK = 256
PAD = 256
HALF = D // 2
NT = (((1,), (1,)), ((), ()))
TN = (((0,), (0,)), ((), ()))
F32 = jnp.float32
BF16 = jnp.bfloat16
MB = 1 << 20


def nn(a, b):
    return jnp.dot(a, b, preferred_element_type=F32)


def nt(a, b):
    return lax.dot_general(a, b, NT, preferred_element_type=F32)


def tn(a, b):
    return lax.dot_general(a, b, TN, preferred_element_type=F32)


def call(body, name, grid, in_specs, out_specs, out_shape, scratch=(), prefetch=0, vmem=48, aliases={}):
    return pl.pallas_call(
        body,
        name=name,
        input_output_aliases=aliases,
        out_shape=out_shape,
        grid_spec=pltpu.PrefetchScalarGridSpec(
            num_scalar_prefetch=prefetch,
            grid=grid,
            in_specs=in_specs,
            out_specs=out_specs,
            scratch_shapes=list(scratch),
        ),
        compiler_params=pltpu.CompilerParams(
            dimension_semantics=("arbitrary",) * len(grid), vmem_limit_bytes=vmem * MB
        ),
        cost_estimate=pl.CostEstimate(flops=1000, bytes_accessed=1000, transcendentals=0),
    )


def rows_spec(cols, offset=0):
    return pl.BlockSpec((BLK, cols), lambda i, *_: (i + offset, 0))


def full_spec(*shape):
    return pl.BlockSpec(shape, lambda *_: (0,) * len(shape))


def by_rows(body):
    @pl.loop(0, BLK // CHUNK)
    def _(i):
        body(pl.ds(pl.multiple_of(i * CHUNK, CHUNK), CHUNK))


def group_spec(count, cols, offset=0):
    return pl.BlockSpec((count, BLK, cols), lambda i, *_: (0, i + offset, 0))


def half_at(index):
    return pl.ds(pl.multiple_of(index * HALF, HALF), HALF)


def place_heads(values, out_ref, g):
    width = values.shape[1] // 3
    rest = jnp.zeros((values.shape[0], PAD - width), BF16)
    for c in range(3):
        out_ref[g, :, c * PAD : c * PAD + width] = values[:, c * width : (c + 1) * width]
        out_ref[g, :, c * PAD + width : (c + 1) * PAD] = rest


def project_first_body(at_ref, x_ref, gain_ref, mine_ref, other_ref, low_ref, out_ref):
    gain = gain_ref[...]

    def norm(rows):
        x = x_ref[rows, :].astype(F32)
        factor = lax.rsqrt(jnp.mean(x * x, axis=-1, keepdims=True) + EPS)
        low_ref[rows, :] = (x * factor * gain).astype(BF16)

    by_rows(norm)
    here, there = half_at(at_ref[0]), half_at(1 - at_ref[0])
    found = nn(low_ref[:, here], mine_ref[...]) + nn(low_ref[:, there], other_ref[...])
    place_heads(found.astype(BF16), out_ref, 0)


def project_first(place, tokens, gain, mine, other):
    rows = tokens.shape[0]
    cols = mine.shape[1]
    return call(
        project_first_body,
        "norm_project",
        (rows // BLK,),
        [rows_spec(D), full_spec(1, D), full_spec(HALF, cols), full_spec(HALF, cols)],
        [rows_spec(D), group_spec(1, 3 * PAD)],
        [jax.ShapeDtypeStruct((rows, D), BF16), jax.ShapeDtypeStruct((1, rows, 3 * PAD), BF16)],
        prefetch=1,
    )(place, tokens, gain, mine, other)


def project_rest_body(at_ref, low_ref, *rest):
    out_ref = rest[-1]
    here, there = half_at(at_ref[0]), half_at(1 - at_ref[0])
    for g in range(out_ref.shape[0]):
        found = nn(low_ref[:, here], rest[2 * g][...]) + nn(low_ref[:, there], rest[2 * g + 1][...])
        place_heads(found.astype(BF16), out_ref, g)


def project_rest(place, low, weights):
    rows = low.shape[0]
    cols = weights[0].shape[1]
    count = len(weights) // 2
    return call(
        project_rest_body,
        "project_rest",
        (rows // BLK,),
        [rows_spec(D)] + [full_spec(HALF, cols)] * len(weights),
        group_spec(count, 3 * PAD),
        jax.ShapeDtypeStruct((count, rows, 3 * PAD), BF16),
        prefetch=1,
    )(place, low, *weights)


TILES = ((0, 0), (0, 1), (1, None))


def heads_of(wide):
    lane = lax.broadcasted_iota(jnp.int32, (wide.shape[0], LANES), 1) < HD
    zero = jnp.zeros((wide.shape[0], LANES), wide.dtype)
    first, second = wide[:, :LANES], wide[:, LANES:]
    return (jnp.where(lane, first, zero), jnp.where(lane, zero, first), second)


def pair_mask(key_block, starts, diagonal):
    key_at = lax.broadcasted_iota(jnp.int32, (BLK, BLK), 0)
    mask = key_at >= starts - key_block * BLK
    if diagonal:
        mask = mask & (key_at <= lax.broadcasted_iota(jnp.int32, (BLK, BLK), 1))
    return mask


def block_at(kb):
    return pl.ds(kb * BLK, BLK) if isinstance(kb, int) else pl.ds(pl.multiple_of(kb * BLK, BLK), BLK)


def tile_of(ref, rows, part, h):
    low = part * PAD + TILES[h][0] * LANES
    return ref[0, rows, low : low + LANES]


def attend_body(low_ref, x_ref, start_ref, o_ref, lse_ref, vt_ref):
    seq = pl.program_id(1)
    for kb in range(QBLOCKS):
        vt_ref[kb] = x_ref[0, kb * BLK : (kb + 1) * BLK, 2 * PAD :].T
    for qb in range(QBLOCKS):
        here = slice(qb * BLK, (qb + 1) * BLK)
        queries = heads_of(x_ref[0, here, :PAD] * jnp.asarray(HD**-0.5, BF16))
        starts = start_ref[0, :, here]

        def scores_of(kb, diagonal):
            mask = pair_mask(kb, starts, diagonal)
            rows = block_at(kb)
            return [
                jnp.where(mask, nt(tile_of(x_ref, rows, 1, h), queries[h]), NEG) for h in range(3)
            ]

        def values_of(kb, h):
            return vt_ref[kb, h * HD : (h + 1) * HD, :]

        blocks = [(qb, scores_of(qb, True))]
        if qb:
            blocks.append((qb - 1, scores_of(qb - 1, False)))
        carry = []
        for h in range(3):
            highest = functools.reduce(
                jnp.maximum, [jnp.max(sc[h], axis=0, keepdims=True) for _, sc in blocks]
            )
            weights = [jnp.exp(sc[h] - highest) for _, sc in blocks]
            total = sum(jnp.sum(w, axis=0, keepdims=True) for w in weights)
            acc = sum(nn(values_of(kb, h), w.astype(BF16)) for (kb, _), w in zip(blocks, weights))
            carry += [highest, total, acc]

        def step(kb, carry):
            scores = scores_of(kb, False)
            out = []
            for h in range(3):
                highest, total, acc = carry[3 * h : 3 * h + 3]
                now = jnp.maximum(highest, jnp.max(scores[h], axis=0, keepdims=True))
                weights = jnp.exp(scores[h] - now)
                fade = jnp.exp(highest - now)
                total = total * fade + jnp.sum(weights, axis=0, keepdims=True)
                out += [now, total, acc * fade + nn(values_of(kb, h), weights.astype(BF16))]
            return tuple(out)

        if qb > 1:
            carry = lax.fori_loop(low_ref[seq * QBLOCKS + qb], qb - 1, step, tuple(carry))
        parts = [carry[3 * h + 2] / carry[3 * h + 1] for h in range(3)]
        parts.append(jnp.zeros((PAD - 3 * HD, BLK), F32))
        o_ref[0, here, :] = jnp.concatenate(parts, axis=0).T.astype(BF16)
        for h in range(3):
            lse_ref[0, 0, h : h + 1, here] = carry[3 * h] + jnp.log(carry[3 * h + 1])


def attend(qkv, starts, lowest):
    groups, rows = qkv.shape[:2]
    seqs = rows // SEQ_LEN
    return call(
        attend_body,
        "attend",
        (groups, seqs),
        [
            pl.BlockSpec((1, SEQ_LEN, 3 * PAD), lambda g, s, *_: (g, s, 0)),
            pl.BlockSpec((1, 1, SEQ_LEN), lambda g, s, *_: (s, 0, 0)),
        ],
        [
            pl.BlockSpec((1, SEQ_LEN, PAD), lambda g, s, *_: (g, s, 0)),
            pl.BlockSpec((1, 1, 3, SEQ_LEN), lambda g, s, *_: (g, s, 0, 0)),
        ],
        [
            jax.ShapeDtypeStruct((groups, rows, PAD), BF16),
            jax.ShapeDtypeStruct((groups, seqs, 3, SEQ_LEN), F32),
        ],
        scratch=[pltpu.VMEM((QBLOCKS, PAD, BLK), BF16)],
        prefetch=1,
    )(lowest, qkv, starts)


def attend_back_body(seq, low_ref, x_ref, start_ref, do_ref, o_ref, lse_ref, g_ref, kt_ref, dk_ref, dv_ref):
    pick = (
        lax.broadcasted_iota(jnp.int32, (8, PAD), 1) // HD
        == lax.broadcasted_iota(jnp.int32, (8, PAD), 0)
    ).astype(F32)
    for kb in range(QBLOCKS):
        kt_ref[kb] = x_ref[0, kb * BLK : (kb + 1) * BLK, PAD : 2 * PAD].T
    for qb in range(QBLOCKS):
        here = slice(qb * BLK, (qb + 1) * BLK)
        queries = heads_of(x_ref[0, here, :PAD] * jnp.asarray(HD**-0.5, BF16))
        upstream = do_ref[0, here, :]
        ups = heads_of(upstream)
        deltas = lax.dot_general(
            pick,
            upstream.astype(F32) * o_ref[0, here, :].astype(F32),
            NT,
            precision=lax.Precision.HIGHEST,
            preferred_element_type=F32,
        )
        starts = start_ref[0, :, here]

        def step(kb, carry, diagonal):
            at = block_at(kb)
            mask = pair_mask(kb, starts, diagonal)
            out, dks, dvs = [], [], []
            for h in range(3):
                scores = jnp.where(mask, nt(tile_of(x_ref, at, 1, h), queries[h]), NEG)
                weights = jnp.exp(scores - lse_ref[0, 0, h : h + 1, here])
                slopes = weights * (nt(tile_of(x_ref, at, 2, h), ups[h]) - deltas[h : h + 1, :])
                slopes = slopes.astype(BF16)
                dvs.append(nn(weights.astype(BF16), ups[h]))
                dks.append(nn(slopes, queries[h]))
                out.append(carry[h] + nn(kt_ref[kb, h * HD : (h + 1) * HD, :], slopes))
            for ref, grads in ((dk_ref, dks), (dv_ref, dvs)):
                if diagonal:
                    ref[at, :LANES] = grads[0] + grads[1]
                    ref[at, LANES:] = grads[2]
                else:
                    ref[at, :LANES] += grads[0] + grads[1]
                    ref[at, LANES:] += grads[2]
            return tuple(out)

        zero = jnp.zeros((HD, BLK), F32)
        carry = step(qb, (zero, zero, zero), True)
        if qb:
            carry = step(qb - 1, carry, False)
        if qb > 1:
            carry = lax.fori_loop(
                low_ref[seq * QBLOCKS + qb], qb - 1, lambda kb, c: step(kb, c, False), carry
            )
        parts = list(carry) + [jnp.zeros((PAD - 3 * HD, BLK), F32)]
        g_ref[0, here, :PAD] = (jnp.concatenate(parts, axis=0) * (HD**-0.5)).T.astype(BF16)
    g_ref[0, :, PAD : 2 * PAD] = dk_ref[...].astype(BF16)
    g_ref[0, :, 2 * PAD :] = dv_ref[...].astype(BF16)


def attend_back(seq, qkv, starts, lowest, grad_out, attended, log_sums):
    groups = qkv.shape[0]

    def block(cols, row):
        return pl.BlockSpec((1, SEQ_LEN, cols), lambda g, *_: (g, row, 0))

    return call(
        functools.partial(attend_back_body, seq),
        "attend_back",
        (groups,),
        [
            block(3 * PAD, seq),
            pl.BlockSpec((1, 1, SEQ_LEN), lambda g, *_: (seq, 0, 0)),
            block(PAD, 0),
            block(PAD, seq),
            pl.BlockSpec((1, 1, 3, SEQ_LEN), lambda g, *_: (g, seq, 0, 0)),
        ],
        block(3 * PAD, 0),
        jax.ShapeDtypeStruct((groups, SEQ_LEN, 3 * PAD), BF16),
        scratch=[
            pltpu.VMEM((QBLOCKS, PAD, BLK), BF16),
            pltpu.VMEM((SEQ_LEN, PAD), F32),
            pltpu.VMEM((SEQ_LEN, PAD), F32),
        ],
        prefetch=1,
    )(lowest, qkv, starts, grad_out, attended, log_sums)


def lane_of(shape):
    return lax.broadcasted_iota(jnp.int32, shape, 1)


def members_of(routes):
    lane = lane_of((routes.shape[0], LANES))
    return ((lane == routes[:, 0:1]) | (lane == routes[:, 1:2])).astype(F32)


def sum_groups(part_ref, rows):
    total = part_ref[0, rows, :]
    for g in range(1, part_ref.shape[0]):
        total = total + part_ref[g, rows, :]
    return total


def group_slot(at_ref, k, groups):
    return lax.rem(at_ref[1] - k + groups, groups)


def middle_body(groups, at_ref, first_ref, rest_ref, x_ref, gain_ref, rw_ref, cv_ref, cot_ref, prev_ref, *refs):
    weights = refs[: 2 * groups]
    after_ref, low_ref, info_ref, part_ref, dot_ref = refs[2 * groups :]
    here, there = half_at(at_ref[0]), half_at(1 - at_ref[0])
    for k in range(groups):
        width = weights[2 * k].shape[0]
        heads = (rest_ref[k - 1] if k else first_ref[0])[:, :width]
        slot = group_slot(at_ref, k, groups)
        part_ref[slot, :, here] = nn(heads, weights[2 * k][...])
        part_ref[slot, :, there] = nn(heads, weights[2 * k + 1][...])
    gain = gain_ref[...]

    def norm(rows):
        after = x_ref[rows, :].astype(F32) + sum_groups(part_ref, rows)
        after_ref[rows, :] = after
        factor = lax.rsqrt(jnp.mean(after * after, axis=-1, keepdims=True) + EPS)
        normed = after * factor * gain
        low_ref[rows, :] = normed.astype(BF16)
        dot = jnp.sum(cot_ref[rows, :].astype(F32) * normed, axis=-1, keepdims=True)
        dot_ref[rows, :] = jnp.broadcast_to(dot, (CHUNK, LANES))

    by_rows(norm)
    products = nt(low_ref[...], rw_ref[...])
    mine, swapped = products[:, :LANES], products[:, LANES:]
    dots = nt(cot_ref[...], cv_ref[...])
    lane = lane_of(mine.shape)
    logits = jnp.where(lane < ALL_EXPERTS, mine + prev_ref[...], NEG)
    grown = jnp.exp(logits - jnp.max(logits, axis=-1, keepdims=True))
    chances = grown / jnp.sum(grown, axis=-1, keepdims=True)
    mixing = 1.0 / (1.0 + jnp.exp(swapped - mine))
    info = jnp.where(lane < 12, chances, jnp.where(lane < 16, mixing, dots))
    info_ref[...] = jnp.where(lane == 18, dot_ref[...], info)


def middle(place, first, rest, weights, tokens, gain, rw, cv, cot, prev):
    rows = tokens.shape[0]
    groups = len(weights) // 2
    return call(
        functools.partial(middle_body, groups),
        "out_norm_route",
        (rows // BLK,),
        [
            group_spec(1, PAD),
            group_spec(groups - 1, PAD),
            rows_spec(D),
            full_spec(1, D),
            full_spec(2 * LANES, D),
            full_spec(LANES, D),
            rows_spec(D),
            rows_spec(LANES),
        ]
        + [full_spec(*w.shape) for w in weights],
        [rows_spec(D), rows_spec(D), rows_spec(LANES)],
        [
            jax.ShapeDtypeStruct((rows, D), F32),
            jax.ShapeDtypeStruct((rows, D), BF16),
            jax.ShapeDtypeStruct((rows, LANES), F32),
        ],
        scratch=[pltpu.VMEM((groups, BLK, D), F32), pltpu.VMEM((BLK, LANES), F32)],
        prefetch=1,
    )(place, first, rest, tokens, gain, rw, cv, cot, prev, *weights)


def dispatch_body(start_ref, rows_ref, rank_ref, out_ref, acc_ref):
    expert = pl.program_id(0)
    acc_ref[...] = jnp.zeros_like(acc_ref)
    blocks = rows_ref.shape[0] // BLK
    for tb in range(blocks):
        here = slice(tb * BLK, (tb + 1) * BLK)
        at = expert * (blocks + 1) + tb
        first = pl.multiple_of(start_ref[at] // 16 * 16, 16)
        slot = lax.broadcasted_iota(jnp.int32, (WIN, BLK), 0)
        chosen = jnp.where(rank_ref[0, :, here] - first == slot, 1.0, 0.0).astype(BF16)
        acc_ref[pl.ds(first, WIN), :] += nn(chosen, rows_ref[here, :]).astype(acc_ref.dtype)
    out_ref[0] = acc_ref[:CAPACITY, :]


def dispatch(rows, ranks, starts, dtype, name):
    count, cols = rows.shape
    experts = ranks.shape[0]
    return call(
        dispatch_body,
        name,
        (experts,),
        [full_spec(count, cols), pl.BlockSpec((1, 1, count), lambda e, *_: (e, 0, 0))],
        pl.BlockSpec((1, CAPACITY, cols), lambda e, *_: (e, 0, 0)),
        jax.ShapeDtypeStruct((experts, CAPACITY, cols), dtype),
        scratch=[pltpu.VMEM((CAPACITY + WIN, cols), dtype)],
        prefetch=1,
    )(starts, rows, ranks)


def combine_body(seq, blocks, start_ref, first_ref, second_ref, rank_ref, info_ref, *rest):
    block = pl.program_id(0)
    out_ref = rest[0]
    dg_ref = rest[1] if len(rest) == 2 else None
    if dg_ref is not None:

        @pl.when(block == 0)
        def _():
            refs = [(first_ref, second_ref)[e % 2].at[e // 2] for e in range(EXPERTS)]
            lines = []
            for r in range(2):
                lines += [ref[CAPACITY + r : CAPACITY + r + 1, :CAPACITY].astype(F32) for ref in refs]
            lines.append(jnp.zeros((LANES - 2 * EXPERTS, CAPACITY), F32))
            dg_ref[...] = jnp.concatenate(lines, axis=0).T.astype(BF16)

    tb = seq * QBLOCKS + pl.program_id(0)
    slot = lax.broadcasted_iota(jnp.int32, (BLK, WIN), 1)
    lane = lane_of((BLK, LANES))
    acc = jnp.zeros((BLK, D), F32)
    picked = jnp.zeros((BLK, LANES), F32)
    for expert in range(EXPERTS):
        rows_ref = (first_ref, second_ref)[expert % 2]
        low = start_ref[expert * (blocks + 1) + tb] // 16 * 16
        first = pl.multiple_of(jnp.minimum(low, CAPACITY - WIN), 16)
        chosen = jnp.where(rank_ref[:, expert : expert + 1] - first == slot, 1.0, 0.0).astype(BF16)
        acc += info_ref[:, expert : expert + 1] * nn(chosen, rows_ref[expert // 2, pl.ds(first, WIN), :])
        if dg_ref is not None:
            mine = (lane == expert) | (lane == EXPERTS + expert)
            got = jnp.where(mine, nn(chosen, dg_ref[pl.ds(first, WIN), :]), 0.0)
            picked += jnp.where(lane == expert, jnp.sum(got, axis=-1, keepdims=True), 0.0)
    if dg_ref is None:
        out_ref[...] = acc.astype(BF16)
    else:
        out_ref[pl.ds(pl.multiple_of(block * BLK, BLK), BLK), :] = acc.astype(BF16)
        dots = picked.T[:EXPERTS].astype(BF16)
        for i in range(QBLOCKS):

            @pl.when(block == i)
            def _():
                row = SEQ_LEN + i // 2 * EXPERTS
                out_ref[row : row + EXPERTS, i % 2 * BLK : (i % 2 + 1) * BLK] = dots

        @pl.when(block == 0)
        def _():
            out_ref[SEQ_LEN:, 2 * BLK :] = jnp.zeros((2 * EXPERTS, D - 2 * BLK), BF16)


def combine(seq, seqs, first, second, rank_cols, info, starts, dots, name):
    count = rank_cols.shape[0]
    blocks = count // BLK
    owners = first.shape[0]
    at = seq * QBLOCKS
    if not dots:
        out, out_spec = jax.ShapeDtypeStruct((seqs * SEQ_LEN, D), BF16), rows_spec(D)
    else:
        out = jax.ShapeDtypeStruct((SEQ_LEN + 2 * EXPERTS, D), BF16)
        out_spec = full_spec(*out.shape)
    return call(
        functools.partial(combine_body, seq, blocks),
        name,
        (seqs * QBLOCKS,),
        [
            full_spec(owners, first.shape[1], D),
            full_spec(owners, first.shape[1], D),
            rows_spec(LANES, at),
            rows_spec(LANES, at),
        ],
        out_spec,
        out,
        scratch=[pltpu.VMEM((CAPACITY, LANES), BF16)] if dots else [],
        prefetch=1,
    )(starts, first, second, rank_cols, info)


def expert_body(x_ref, c_ref, gu_ref, dn_ref, act_ref, both_ref, dx_ref):
    hidden = dn_ref.shape[0]
    both = nn(x_ref[0], gu_ref[...])
    gate, up = both[:, :hidden], both[:, hidden:]
    sig = jax.nn.sigmoid(gate)
    act = (gate * sig * up).astype(BF16)
    act_ref[0] = act
    grad_act = nt(c_ref[0], dn_ref[...])
    dots = jnp.sum(act.astype(F32) * grad_act, axis=-1, keepdims=True)
    dots = jnp.broadcast_to(dots, (CAPACITY, LANES)).T[:16]
    high = dots.astype(BF16).astype(F32)
    dots = jnp.where(lax.broadcasted_iota(jnp.int32, dots.shape, 0) == 0, high, dots - high)
    grad_gate = grad_act * up * sig * (1.0 + gate * (1.0 - sig))
    grad_up = grad_act * (gate * sig)
    grad_both = jnp.concatenate([grad_gate, grad_up], axis=-1).astype(BF16)
    both_ref[0] = grad_both
    dx_ref[0, :CAPACITY, :] = nt(grad_both, gu_ref[...]).astype(BF16)
    dots = jnp.concatenate([dots, jnp.zeros((16, D - CAPACITY), F32)], axis=1)
    dx_ref[0, CAPACITY:, :] = dots.astype(BF16)


def expert_core(x, cot, gate_up, down):
    sources = x.shape[0]
    hidden = down.shape[0]

    def block(cols):
        return pl.BlockSpec((1, CAPACITY, cols), lambda s: (s, 0, 0))

    return call(
        expert_body,
        "expert",
        (sources,),
        [block(D), block(D), full_spec(D, 2 * hidden), full_spec(hidden, D)],
        [block(hidden), block(2 * hidden), pl.BlockSpec((1, SENT, D), lambda s: (s, 0, 0))],
        [
            jax.ShapeDtypeStruct((sources, CAPACITY, hidden), BF16),
            jax.ShapeDtypeStruct((sources, CAPACITY, 2 * hidden), BF16),
            jax.ShapeDtypeStruct((sources, SENT, D), BF16),
        ],
    )(x, cot, gate_up, down)


def output_body(after_ref, moe_ref, info_ref, routes_ref, gain_ref, cv_ref, out_ref):
    gain = gain_ref[...]

    def finish(rows):
        after = after_ref[rows, :]
        factor = lax.rsqrt(jnp.mean(after * after, axis=-1, keepdims=True) + EPS)
        info = info_ref[rows, :]
        gates = info * members_of(routes_ref[rows, :])
        coef = gates[:, 9:10] + gates[:, 10:11] * info[:, 12:13] + gates[:, 11:12] * info[:, 14:15]
        out = after * (1.0 + (coef * factor) * gain) + moe_ref[rows, :].astype(F32)
        out = out + (gates[:, 10:11] * info[:, 13:14]) * cv_ref[0:1, :]
        out_ref[rows, :] = out + (gates[:, 11:12] * info[:, 15:16]) * cv_ref[1:2, :]

    by_rows(finish)


def finish_output(after, moe, info, routes, gain, cv):
    rows = after.shape[0]
    return call(
        output_body,
        "output",
        (rows // BLK,),
        [rows_spec(D), rows_spec(D), rows_spec(LANES), rows_spec(2), full_spec(1, D), full_spec(2, D)],
        rows_spec(D),
        jax.ShapeDtypeStruct((rows, D), F32),
    )(after, moe, info, routes, gain, cv)


def back_body(groups, at_ref, after_ref, cot_ref, moe_ref, info_ref, dg_ref, routes_ref, gain_ref, rw_ref, low_ref, *refs):
    weights = refs[: 2 * groups]
    grad_ref, glow_ref, first_ref, rest_ref, small_ref, routed_ref, coef_ref, sum_ref = refs[2 * groups :]
    block = pl.program_id(0)

    @pl.when(block == 0)
    def _():
        small_ref[...] = jnp.zeros_like(small_ref)
        sum_ref[...] = jnp.zeros_like(sum_ref)

    info = info_ref[...]
    members = members_of(routes_ref[...])
    gates = info * members
    lane = lane_of(info.shape)
    dot_normed = info[:, 18:19]
    dots = dg_ref[:, pl.ds(pl.multiple_of(block % 2 * BLK, BLK), BLK)].astype(F32)
    dots = jnp.where(block < 2, dots[:EXPERTS], dots[EXPERTS:])
    dots = jnp.concatenate([dots, jnp.zeros((LANES - EXPERTS, BLK), F32)], axis=0).T
    grad = jnp.where(lane < EXPERTS, dots, 0.0)
    grad = grad + jnp.where(lane == 9, dot_normed, 0.0)
    grad_mix = jnp.zeros_like(grad)
    coef = gates[:, 9:10]
    coefs = jnp.zeros_like(grad)
    for c in range(2):
        first, second = info[:, 12 + 2 * c : 13 + 2 * c], info[:, 13 + 2 * c : 14 + 2 * c]
        dot_const = info[:, 16 + c : 17 + c]
        weight = gates[:, 10 + c : 11 + c]
        inner = first * dot_normed + second * dot_const
        grad = grad + jnp.where(lane == 10 + c, inner, 0.0)
        grad_mix = grad_mix + jnp.where(lane == 12 + 2 * c, first * weight * (dot_normed - inner), 0.0)
        grad_mix = grad_mix + jnp.where(lane == 13 + 2 * c, second * weight * (dot_const - inner), 0.0)
        coef = coef + weight * first
        coefs = coefs + jnp.where(lane == 1 + c, weight * second, 0.0)
    coef_ref[...] = coefs + jnp.where(lane == 0, coef, 0.0)
    grad = grad * members
    chances = jnp.where(lane < ALL_EXPERTS, info, 0.0)
    grad_logits = chances * (grad - jnp.sum(chances * grad, axis=-1, keepdims=True))
    slopes = (grad_logits + grad_mix).astype(BF16)
    routed_ref[...] = nn(slopes, rw_ref[...])
    small_ref[0:16, :] += tn(slopes, low_ref[...])[:16, :]
    gain = gain_ref[...]

    def norm(rows):
        after = after_ref[rows, :]
        cot = cot_ref[rows, :].astype(F32)
        columns = coef_ref[rows, :]
        factor = lax.rsqrt(jnp.mean(after * after, axis=-1, keepdims=True) + EPS)
        xhat = after * factor
        grad_normed = columns[:, 0:1] * cot + routed_ref[rows, :] + moe_ref[rows, :].astype(F32)
        weighted = grad_normed * gain
        inner = jnp.mean(weighted * xhat, axis=-1, keepdims=True)
        grad_after = cot + factor * (weighted - xhat * inner)
        grad_ref[rows, :] = grad_after
        glow_ref[rows, :] = grad_after.astype(BF16)
        for i, value in enumerate((grad_normed * xhat, columns[:, 1:2] * cot, columns[:, 2:3] * cot)):
            total = value[0:8]
            for r in range(8, CHUNK, 8):
                total = total + value[r : r + 8]
            sum_ref[i] += total

    by_rows(norm)
    here, there = half_at(at_ref[0]), half_at(1 - at_ref[0])
    for k in range(groups):
        grad_heads = nt(glow_ref[:, here], weights[2 * k][...]) + nt(glow_ref[:, there], weights[2 * k + 1][...])
        width = grad_heads.shape[1]
        ref, g = (rest_ref, k - 1) if k else (first_ref, 0)
        ref[g, :, :width] = grad_heads.astype(BF16)
        ref[g, :, width:] = jnp.zeros((BLK, PAD - width), BF16)

    @pl.when(block == pl.num_programs(0) - 1)
    def _():
        for i in range(3):
            small_ref[16 + i : 17 + i, :] = jnp.sum(sum_ref[i], axis=0, keepdims=True)


def back(seq, place, after, cot, moe, info, routes, gain, rw, low, weights):
    at = seq * QBLOCKS
    groups = len(weights) // 2
    return call(
        functools.partial(back_body, groups),
        "route_norm_back",
        (QBLOCKS,),
        [
            rows_spec(D, at),
            rows_spec(D, at),
            rows_spec(D),
            rows_spec(LANES, at),
            pl.BlockSpec((2 * EXPERTS, D), lambda i, *_: (SEQ_LEN // (2 * EXPERTS), 0)),
            rows_spec(2, at),
            full_spec(1, D),
            full_spec(LANES, D),
            rows_spec(D, at),
        ]
        + [full_spec(*w.shape) for w in weights],
        [rows_spec(D), rows_spec(D), group_spec(1, PAD), group_spec(groups - 1, PAD), full_spec(24, D)],
        [
            jax.ShapeDtypeStruct((SEQ_LEN, D), F32),
            jax.ShapeDtypeStruct((SEQ_LEN, D), BF16),
            jax.ShapeDtypeStruct((1, SEQ_LEN, PAD), BF16),
            jax.ShapeDtypeStruct((groups - 1, SEQ_LEN, PAD), BF16),
            jax.ShapeDtypeStruct((24, D), F32),
        ],
        scratch=[pltpu.VMEM((BLK, D), F32), pltpu.VMEM((BLK, LANES), F32), pltpu.VMEM((3, 8, D), F32)],
        prefetch=1,
    )(place, after, cot, moe, info, moe, routes, gain, rw, low, *weights)


def final_body(groups, at_ref, first_ref, rest_ref, x_ref, gain_ref, after_ref, *refs):
    weights = refs[: 2 * groups]
    out_ref, small_ref, part_ref, sum_ref = refs[-4:]
    here, there = half_at(at_ref[0]), half_at(1 - at_ref[0])
    for k in range(groups):
        wide = rest_ref[k - 1] if k else first_ref[0]
        width = weights[2 * k].shape[1] // 3
        packed = jnp.concatenate([wide[:, c * PAD : c * PAD + width] for c in range(3)], axis=1)
        slot = group_slot(at_ref, k, groups)
        part_ref[slot, :, here] = nt(packed, weights[2 * k][...])
        part_ref[slot, :, there] = nt(packed, weights[2 * k + 1][...])

    @pl.when(pl.program_id(0) == 0)
    def _():
        sum_ref[...] = jnp.zeros_like(sum_ref)

    gain = gain_ref[...]

    def norm(rows):
        grad = sum_groups(part_ref, rows)
        x = x_ref[rows, :].astype(F32)
        factor = lax.rsqrt(jnp.mean(x * x, axis=-1, keepdims=True) + EPS)
        xhat = x * factor
        weighted = grad * gain
        inner = jnp.mean(weighted * xhat, axis=-1, keepdims=True)
        out_ref[rows, :] = after_ref[rows, :] + factor * (weighted - xhat * inner)
        value = grad * xhat
        total = value[0:8]
        for r in range(8, CHUNK, 8):
            total = total + value[r : r + 8]
        sum_ref[...] += total

    by_rows(norm)
    small_ref[...] = sum_ref[...]


def final(seq, place, first, rest, weights, tokens, gain, grad_after, earlier):
    rows = tokens.shape[0]
    at = seq * QBLOCKS
    groups = len(weights) // 2
    extra = [] if earlier is None else [earlier]
    return call(
        functools.partial(final_body, groups),
        "norm_back",
        (QBLOCKS,),
        [
            group_spec(1, 3 * PAD),
            group_spec(groups - 1, 3 * PAD),
            rows_spec(D, at),
            full_spec(1, D),
            rows_spec(D),
        ]
        + [full_spec(*w.shape) for w in weights]
        + [pl.BlockSpec(memory_space=pl.ANY)] * len(extra),
        [rows_spec(D, at), full_spec(8, D)],
        [jax.ShapeDtypeStruct((rows, D), F32), jax.ShapeDtypeStruct((8, D), F32)],
        scratch=[pltpu.VMEM((groups, BLK, D), F32), pltpu.VMEM((8, D), F32)],
        prefetch=1,
        aliases={6 + len(weights): 0} if extra else {},
    )(place, first, rest, tokens, gain, grad_after, *weights, *extra)


def gather_dp(x, axis):
    n = lax.axis_size("dp")
    if n != 2:
        return lax.all_gather(x, "dp", axis=axis, tiled=True)
    other = lax.ppermute(x, "dp", [(0, 1), (1, 0)])
    here = lax.axis_index("dp") == 0
    return jnp.concatenate([jnp.where(here, x, other), jnp.where(here, other, x)], axis=axis)


def scatter_dp(x, axis):
    n = lax.axis_size("dp")
    if n != 2:
        return lax.psum_scatter(x.astype(BF16), "dp", scatter_dimension=axis, tiled=True).astype(F32)
    half = x.shape[axis] // 2
    me = lax.axis_index("dp")
    keep = lax.dynamic_slice_in_dim(x, me * half, half, axis)
    send = lax.dynamic_slice_in_dim(x, (1 - me) * half, half, axis).astype(BF16)
    return keep.astype(F32) + lax.ppermute(send, "dp", [(0, 1), (1, 0)]).astype(F32)


def sum_over(x, axis_name):
    n = lax.axis_size(axis_name)
    if n & (n - 1):
        return lax.psum(x.astype(BF16), axis_name).astype(F32)
    step = 1
    while step < n:
        low = x.astype(BF16)
        other = lax.ppermute(low, axis_name, [(i, i ^ step) for i in range(n)])
        x = low.astype(F32) + other.astype(F32)
        step *= 2
    return x


def shifted(x):
    n = lax.axis_size("tensor")
    return [lax.ppermute(x, "tensor", [(i, (i + k) % n) for i in range(n)]) for k in range(1, n)]


def halves(x, axis):
    if lax.axis_size("dp") == 2:
        return [x, lax.ppermute(x, "dp", [(0, 1), (1, 0)])]
    return jnp.split(lax.all_gather(x, "dp", axis=axis, tiled=True), 2, axis=axis)


def join(part, other):
    return (part.astype(F32) + other.astype(F32)).astype(BF16)


def to_inner(part):
    return join(part, lax.ppermute(part, "tensor", [(0, 1), (3, 2)]))


def between_inner(part):
    return join(part, lax.ppermute(part, "tensor", [(1, 2), (2, 1)]))


def to_outer(part):
    me = lax.axis_index("tensor")
    other = lax.ppermute(part, "tensor", [(1, 0), (2, 3)])
    return jnp.where((me == 0) | (me == 3), other, part)


def exchange_small(x):
    n = lax.axis_size("expert")
    me = lax.axis_index("expert")
    return jnp.stack(
        [
            lax.ppermute(
                lax.dynamic_index_in_dim(x, me ^ k, 0, keepdims=False),
                "expert",
                [(i, i ^ k) for i in range(n)],
            )
            if k
            else lax.dynamic_index_in_dim(x, me, 0, keepdims=False)
            for k in range(n)
        ]
    )


def exchange(x):
    return lax.all_to_all(x, "expert", split_axis=0, concat_axis=0, tiled=True)


def route_tables(routes):
    count = routes.shape[0]
    blocks = count // BLK
    ids = jnp.arange(EXPERTS, dtype=jnp.int32)[:, None]
    member = (routes[:, 0][None, :] == ids) | (routes[:, 1][None, :] == ids)
    ones = member.astype(BF16).reshape(EXPERTS, blocks, BLK)
    earlier = (jnp.arange(BLK)[:, None] < jnp.arange(BLK)[None, :]).astype(BF16)
    inside = jnp.einsum("ebt,tu->ebu", ones, earlier, preferred_element_type=F32)
    counts = jnp.sum(ones.astype(F32), axis=-1)
    ends = jnp.cumsum(counts, axis=1)
    starts = ends - counts
    ranks = (inside + starts[:, :, None]).astype(jnp.int32).reshape(EXPERTS, count)
    ranks = jnp.where(member, ranks, -(1 << 20))
    bounds = jnp.concatenate([starts, ends[:, -1:]], axis=1)
    return (ranks, bounds.astype(jnp.int32))


def document_tables(segments):
    seqs = segments.shape[0] // SEQ_LEN
    marks = segments.reshape(seqs, SEQ_LEN // DOC_BLOCK, DOC_BLOCK)[:, :, 0]
    begin = DOC_BLOCK * jnp.sum((marks[:, None, :] < marks[:, :, None]).astype(jnp.int32), axis=-1)
    starts = jnp.broadcast_to(begin[:, :, None], begin.shape + (DOC_BLOCK,)).reshape(seqs, 1, SEQ_LEN)
    lowest = begin[:, :: BLK // DOC_BLOCK] // BLK
    return (starts, lowest.reshape(-1))


def three_parts(x):
    high = x.astype(BF16)
    rest = x - high.astype(F32)
    mid = rest.astype(BF16)
    return (high, mid, (rest - mid.astype(F32)).astype(BF16))


def on_device(
    tokens,
    prev_logits,
    routes,
    segments,
    gain_one,
    w_qkv,
    w_out,
    gain_two,
    router,
    const_proj,
    const_vec,
    w_gate_up,
    w_down,
    cotangent,
):
    rows = tokens.shape[0]
    owners = lax.axis_size("expert")
    groups = lax.axis_size("tensor")
    group = lax.axis_index("tensor")
    local_experts = EXPERTS // owners
    width = w_out.shape[0]
    slice_rows = w_qkv.shape[0]

    own_in = w_qkv.astype(BF16).reshape(slice_rows, 3 * width)
    rest_in = shifted(own_in)
    in_first = halves(own_in, 0)
    dp_at = lax.axis_index("dp") if lax.axis_size("dp") == 2 else jnp.int32(0)
    place = jnp.stack([dp_at, group]).astype(jnp.int32)
    small = jnp.concatenate(
        [router.T, const_proj.T, gain_one[None], gain_two[None], const_vec], axis=0
    ).astype(BF16)
    small = gather_dp(small, 1)
    gain_a = small[16:17].astype(F32)
    gain_b = small[17:18].astype(F32)
    const_rows = small[18:20].astype(F32)
    mains = jnp.pad(small[:16], ((0, LANES - 16), (0, 0)))
    swaps = jnp.stack([small[13], small[12], small[15], small[14]])
    routing = jnp.concatenate([mains, jnp.pad(swaps, ((12, LANES - 16), (0, 0)))], axis=0)
    const_low = jnp.pad(small[18:20], ((16, LANES - 18), (0, 0)))

    ranks, block_starts = route_tables(routes)
    rank_cols = jnp.pad(ranks.T, ((0, 0), (0, LANES - EXPERTS)))
    per_expert = ranks.reshape(owners, local_experts, 1, rows)
    per_start = block_starts.reshape(owners, local_experts, -1)
    table = [
        (per_expert[:, j], per_start[:, j].reshape(-1)) for j in range(local_experts)
    ]
    cot_in = [exchange(dispatch(cotangent, *table[0], BF16, "send_cot"))]
    me = lax.axis_index("expert")
    all_starts = block_starts.reshape(-1)

    hidden = w_down.shape[1]
    gate_up = gather_dp(w_gate_up.astype(BF16).reshape(local_experts, slice_rows, 2 * hidden), 1)
    down = gather_dp(w_down.astype(BF16), 2)

    starts, lowest = document_tables(segments)
    normed_low, qkv_first = project_first(place, tokens, gain_a, *in_first)
    attended_first, sums_first = attend(qkv_first, starts, lowest)
    out_master = w_out.astype(BF16)
    cot_late, attended_first, rest_in, out_master = lax.optimization_barrier(
        (cotangent, attended_first, rest_in, out_master)
    )
    in_rest = sum([halves(w, 0) for w in rest_in], [])
    in_all = in_first + in_rest
    out_all = sum([halves(w, 1) for w in [out_master] + shifted(out_master)], [])
    for j in range(1, local_experts):
        cot_in.append(exchange(dispatch(cot_late, *table[j], BF16, "send_cot")))
    qkv_rest = project_rest(place, normed_low, in_rest)
    attended_rest, sums_rest = attend(qkv_rest, starts, lowest)
    prev = jnp.pad(prev_logits, ((0, 0), (0, LANES - ALL_EXPERTS)))
    after_attn, routed_low, info = middle(
        place,
        attended_first,
        attended_rest,
        out_all,
        tokens,
        gain_b,
        routing,
        const_low,
        cotangent,
        prev,
    )

    routed_low, cot_in = lax.optimization_barrier((routed_low, cot_in))

    rows_in = [exchange(dispatch(routed_low, r, s, BF16, "send_rows")) for r, s in table]
    acts, boths, back_rows = [], [], []
    for j in range(local_experts):
        act, both, grad_rows = expert_core(rows_in[j], cot_in[j], gate_up[j], down[j])
        acts.append(act)
        boths.append(both)
        back_rows.append(exchange(grad_rows))
    seqs = rows // SEQ_LEN

    chance_parts = jnp.concatenate(
        [jnp.pad(p, ((0, 0), (0, 8))) for p in three_parts(info[:, :EXPERTS])], axis=1
    )
    chance_parts = jnp.pad(chance_parts, ((0, 0), (0, LANES - 48)))
    gates = []
    for j in range(local_experts):
        sent = dispatch(chance_parts, *table[j], F32, "send_gates")
        ids = local_experts * jnp.arange(owners)[:, None] + j
        mine = (jnp.arange(LANES)[None, :] % 16 == ids) & (jnp.arange(LANES)[None, :] < 48)
        gates.append(jnp.sum(jnp.where(mine[:, None, :], sent, 0.0), axis=-1))
    outs = [
        jnp.einsum("scf,fd->scd", acts[j], down[j], preferred_element_type=F32).astype(BF16)
        for j in range(local_experts)
    ]
    gates = jnp.stack(gates, axis=1)
    gates, back_rows = lax.optimization_barrier((gates, back_rows))
    gates = exchange_small(gates)
    gates = jnp.take(gates, me ^ jnp.arange(owners), axis=0)
    outs, back_rows = lax.optimization_barrier((outs, back_rows))
    grad_moe = []
    for seq in range(seqs):
        grad_part = combine(
            seq, 1, back_rows[0], back_rows[1], rank_cols, info, all_starts, True, "combine_grads"
        )
        half = SEQ_LEN // 2
        parts = [to_inner(p) for p in (grad_part[:half], grad_part[half:])]
        parts = [to_outer(between_inner(p)) for p in parts]
        grad_moe.append(jnp.concatenate(parts, axis=0))
    outs_back = [exchange(o) for o in outs]
    out_part = combine(
        0, seqs, outs_back[0], outs_back[1], rank_cols, info, all_starts, False, "combine_out"
    )

    out_sums = jnp.split(out_part, 4)

    grad_tokens = None
    grad_dense = small_grads = gain_grads = 0.0
    waiting = []
    grad_qkv = outs_back[0]
    for seq in range(seqs):
        if seq == 0:
            grad_moe[seq], grad_qkv = lax.optimization_barrier((grad_moe[seq], grad_qkv))
        else:
            grad_moe[seq], grad_qkv, out_sums[:2] = lax.optimization_barrier((grad_moe[seq], grad_qkv, out_sums[:2]))
            out_sums[:2] = [between_inner(p) for p in out_sums[:2]]
        grad_after, grad_low, att_first, att_rest, small_part = back(
            seq, place, after_attn, cotangent, grad_moe[seq], info, routes, gain_b, mains, routed_low, out_all
        )
        if seq == 0:
            att_first, att_rest, out_sums = lax.optimization_barrier((att_first, att_rest, out_sums))
            out_sums = [to_inner(p) for p in out_sums]
        here = slice(seq * SEQ_LEN, (seq + 1) * SEQ_LEN)
        grad_first = attend_back(seq, qkv_first, starts, lowest, att_first, attended_first, sums_first)
        grad_dense = grad_dense + jnp.concatenate(
            [
                jnp.einsum("td,tm->dm", normed_low[here], grad_first[0], preferred_element_type=F32),
                jnp.einsum("td,tm->dm", grad_low, attended_first[0, here], preferred_element_type=F32),
            ],
            axis=1,
        )
        small_grads = small_grads + small_part
        if seq == seqs - 1:
            grad_dense, att_rest, out_sums[0], out_sums[2] = lax.optimization_barrier(
                (grad_dense, att_rest, out_sums[0], out_sums[2])
            )
            out_sums[0] = to_outer(out_sums[0])
            out_sums[2] = between_inner(out_sums[2])
        grad_qkv = attend_back(seq, qkv_rest, starts, lowest, att_rest, attended_rest, sums_rest)
        waiting.append((grad_first, grad_qkv, grad_after))

    pieces = [grad_dense[:, c * PAD : c * PAD + width] for c in range(4)]
    grad_dense = scatter_dp(jnp.concatenate(pieces, axis=1), 0)
    small_grads = scatter_dp(small_grads, 1)
    for seq in range(seqs):
        if seq == 0:
            waiting[0], grad_dense, small_grads, out_sums[1:] = lax.optimization_barrier(
                (waiting[0], grad_dense, small_grads, out_sums[1:])
            )
            out_sums[3] = between_inner(out_sums[3])
            out_sums[1:3] = [to_outer(p) for p in out_sums[1:3]]
        if seq == seqs - 1:
            waiting[seq], out_sums[3] = lax.optimization_barrier((waiting[seq], out_sums[3]))
            out_sums[3] = to_outer(out_sums[3])
        grad_first, grad_qkv, grad_after = waiting[seq]
        grad_tokens, gain_part = final(
            seq, place, grad_first, grad_qkv, in_all, tokens, gain_a, grad_after, grad_tokens
        )
        gain_grads = gain_grads + gain_part
    grad_dense = sum_over(grad_dense, "expert")
    small_grads = sum_over(small_grads, "expert")

    output = finish_output(
        after_attn, jnp.concatenate(out_sums, axis=0), info, routes, gain_b, const_rows
    )

    grad_gate_up, grad_down = [], []
    for j in range(local_experts):
        gate = gates[:, j, :, None]
        gated = (gate * boths[j].astype(F32)).astype(BF16)
        gated_cot = (gate * cot_in[j].astype(F32)).astype(BF16)
        grad_gate_up.append(
            jnp.einsum("scd,scf->df", rows_in[j], gated, preferred_element_type=F32)
        )
        grad_down.append(
            jnp.einsum("scf,scd->fd", acts[j], gated_cot, preferred_element_type=F32)
        )
    grad_gate_up = scatter_dp(jnp.stack(grad_gate_up), 1).reshape(w_gate_up.shape)
    grad_down = scatter_dp(jnp.stack(grad_down), 2)

    gain_grads = sum_over(scatter_dp(jnp.sum(gain_grads, axis=0, keepdims=True), 1), "expert")
    return (
        output,
        grad_tokens,
        gain_grads[0],
        grad_dense[:, : 3 * width].reshape(w_qkv.shape),
        grad_dense[:, 3 * width :].T,
        small_grads[16],
        small_grads[:12].T,
        small_grads[12:16].T,
        small_grads[17:19],
        grad_gate_up,
        grad_down,
    )


def solution(mesh):
    token_spec = P(("dp", "expert"), None)
    weight_specs = (
        P("dp"),
        P("dp", None, "tensor"),
        P("tensor", "dp"),
        P("dp"),
        P("dp", None),
        P("dp", None),
        P(None, "dp"),
        P("expert", "dp", None, "tensor"),
        P("expert", "tensor", "dp"),
    )
    return jax.shard_map(
        on_device,
        mesh=mesh,
        in_specs=(token_spec, token_spec, token_spec, P(("dp", "expert"))) + weight_specs + (token_spec,),
        out_specs=(token_spec, token_spec) + weight_specs,
        check_vma=False,
    )
```
